256 devices in a mesh: seq: 64 (over z, y, core), tp: 4 (over x).
Axes of the slice: x: 4, y: 4, z: 8, core: 2. Of those that a mesh axis runs over, the one named last changes fastest.
Arguments:
- tokens: bfloat16 [128, 1536], replicated, may hold values from -6 to 6
- attn_gain: float32 [1536], replicated, may hold values from 0.25 to 1.75
- qkv_weight: bfloat16 [1536, 2560], P(None, 'tp'), may hold values from -0.15625 to 0.15625
- out_weight: bfloat16 [1536, 1536], P(None, 'tp'), may hold values from -0.15625 to 0.15625
- moe_gain: float32 [1536], P('tp'), may hold values from 0.25 to 1.75
- router_weight: bfloat16 [1536, 40], P('tp'), may hold values from -0.3125 to 0.3125
- expert_gate: bfloat16 [40, 1536, 512], P(None, 'tp', 'seq'), may hold values from -0.15625 to 0.15625
- expert_up: bfloat16 [40, 1536, 512], P(None, 'tp', 'seq'), may hold values from -0.15625 to 0.15625
- expert_down: bfloat16 [40, 512, 1536], P(None, 'seq', 'tp'), may hold values from -0.375 to 0.375
- cache_keys: bfloat16 [32, 2048, 512], P(None, 'seq', 'tp'), may hold values from -240 to 240, as said below
- cache_values: bfloat16 [32, 2048, 512], P(None, 'seq', 'tp'), may hold values from -8 to 8
- lengths: int32 [32], replicated, may hold values from 1 to 32768, as said below
- routes: int32 [128, 8], replicated, may hold values from 0 to 39, all different within a row
Outputs:
- layer_out: bfloat16 [128, 1536], P(None, 'tp')
The draws below stay inside these ranges and needn't reach their ends.
Inputs may be any that keep to these rules, and one draw needn't show every extreme that they name: `lengths`: one request has exactly 32768 cached positions. `cache_keys`: cached keys are already rotated.
All inputs are finite; a program needn't handle non-finite values.
Results may differ from the reference program's by a relative error of at most 0.014.
Values may be sent and summed in bfloat16 or wider, within the bound.
No kernel may reach another device: no remote copies, remote signals or barrier semaphores. Data moves between devices by JAX's collectives and lax.ppermute only.
A program may use at most 128 MiB of HBM per device.

```python
import jax
import jax.numpy as jnp
from jax import lax

D = 1536
HEADS = 24
KV_HEADS = 8
HEAD = 64
EXPERTS = 40
FF_E = 512
TOP = 8
SINK = 4
NEW = 4
MAXLEN = 32768
REQS = 32
GROUP = 3
CACHE = 2048
WINDOW = 2044
TOKENS = 128


def draw_cache_keys(key, part):
    base = jax.random.truncated_normal(key, -6.0, 6.0, (REQS, CACHE, KV_HEADS * HEAD), jnp.float32)
    return base.astype(jnp.bfloat16)


def draw_cache_values(key, part):
    slope = (jnp.arange(CACHE, dtype=jnp.float32) * (2.0 / (CACHE - 1)) - 1.0)[None, :, None]
    signs = jnp.where(jax.random.uniform(jax.random.fold_in(key, 3), (REQS, 1, KV_HEADS * HEAD)) < 0.5, -1.0, 1.0)
    base = jax.random.truncated_normal(key, -5.0, 5.0, (REQS, CACHE, KV_HEADS * HEAD), jnp.float32)
    amount = jnp.full((REQS, 1, KV_HEADS * HEAD), 1.5, jnp.float32)
    return (base + amount * slope * signs).astype(jnp.bfloat16)


def draw_lengths(key, part):
    exponents = jax.random.randint(jax.random.fold_in(key, 1), (REQS,), 1, 16)
    upper = jnp.left_shift(jnp.ones((REQS,), jnp.int32), exponents) + 1
    drawn = jax.random.randint(jax.random.fold_in(key, 2), (REQS,), 1, upper)
    return drawn.at[0].set(MAXLEN).astype(jnp.int32)


def level_of(own_key, dims, pieces, least, high):
    level = 1.0
    for axis_at, shards_of in pieces:
        draws = jax.random.uniform(jax.random.fold_in(jax.random.fold_in(own_key, 6), axis_at), (shards_of,), jnp.float32, least / len(pieces), high / len(pieces))
        level = level * jnp.repeat(jnp.exp(draws), dims[axis_at] // shards_of).reshape((-1,) + (1,) * (len(dims) - 1 - axis_at))
    return level


def choose_distinct(key, rows, number_of, top, lift):
    sequence = jax.random.permutation(jax.random.fold_in(key, 1), number_of)
    boost = sequence
    for power in range(3):
        boost = boost * boost // number_of
    boost = boost * lift // number_of
    chance = jax.random.randint(jax.random.fold_in(key, 2), (rows, number_of), 0, 4096) + boost
    sure = jax.random.permutation(jax.random.fold_in(key, 3), rows)[jnp.arange(number_of) % rows]
    chance = jnp.where(jnp.arange(rows)[:, None] == sure[None, :], 1 << 14, chance)
    priority = chance * number_of + jnp.arange(number_of)
    return lax.top_k(priority.astype(jnp.int32), top)[1].astype(jnp.int32)


def centred(own_key, extent, width, most, split=(), kind=jnp.bfloat16):
    loudness = level_of(own_key, extent, split, -0.22, 0.18) if split else 1.0
    result = jax.random.normal(own_key, extent, jnp.float32) * width * loudness
    return jnp.minimum(jnp.maximum(result, -most), most).astype(kind)


def setup_inputs(seed: int = 0) -> dict:
    keys = jax.random.split(jax.random.key(seed), 14)
    return {
        "tokens": centred(keys[0], (TOKENS, D), 1.0, 6.0),
        "attn_gain": jnp.clip(1.0 + 0.15 * jax.random.normal(keys[1], (D,), jnp.float32), 0.25, 1.75),
        "qkv_weight": centred(keys[2], (D, KV_HEADS * (GROUP + 2) * HEAD), D ** -0.5, 0.15625, ((1, 4),)),
        "out_weight": centred(keys[3], (HEADS * HEAD, D), (HEADS * HEAD) ** -0.5, 0.15625, ((1, 4),)),
        "moe_gain": jnp.clip(1.0 + 0.15 * jax.random.normal(keys[4], (D,), jnp.float32), 0.25, 1.75),
        "router_weight": centred(keys[5], (D, EXPERTS), (D // 4) ** -0.5, 0.3125, ((0, 4),)),
        "expert_gate": centred(keys[6], (EXPERTS, D, FF_E), D ** -0.5, 0.15625, ((1, 4), (2, 64))),
        "expert_up": centred(keys[7], (EXPERTS, D, FF_E), D ** -0.5, 0.15625, ((1, 4), (2, 64))),
        "expert_down": centred(keys[8], (EXPERTS, FF_E, D), (FF_E // 2) ** -0.5, 0.375, ((1, 64), (2, 4))),
        "cache_keys": draw_cache_keys(jax.random.fold_in(keys[13], 71), 0),
        "cache_values": draw_cache_values(jax.random.fold_in(keys[13], 71), 0),
        "lengths": draw_lengths(jax.random.fold_in(keys[13], 71), 0),
        "routes": choose_distinct(keys[12], TOKENS, EXPERTS, TOP, 1638),
    }


EPSILON = 1e-06
ROPE_BASE = 10000.0

def rms_scale(values, gain):
    return values * lax.rsqrt(lax.optimization_barrier(jnp.mean(values * values, axis=-1, keepdims=True)) + EPSILON) * gain

def rotate(values, places):
    half_dim = values.shape[-1] // 2
    freqs = jnp.exp(-jnp.log(ROPE_BASE) * jnp.arange(half_dim, dtype=jnp.float32) / half_dim)
    angles = places.reshape((-1,) + (1,) * (values.ndim - 1)) * freqs
    cosine = jnp.cos(angles)
    sine = jnp.sin(angles)
    first = values[..., :half_dim]
    second = values[..., half_dim:]
    return jnp.concatenate([first * cosine - second * sine, first * sine + second * cosine], axis=-1)

def visible(slots, lengths, window):
    lens = lengths[:, None].astype(jnp.int32)
    slot_row = slots[None, :].astype(jnp.int32)
    live = slot_row < lens
    older = lens - 1 - jnp.mod(lens - 1 - slot_row, window)
    placed = jnp.where(slot_row < SINK, slot_row, older)
    offsets = jnp.arange(NEW, dtype=jnp.int32)
    inside = (slot_row[:, None, :] < SINK) | (placed[:, None, :] >= lens[:, :, None] + offsets[None, :, None] - window)
    return live[:, None, :] & inside

def reference(tokens, attn_gain, qkv_weight, out_weight, moe_gain, router_weight, expert_gate, expert_up, expert_down, cache_keys, cache_values, lengths, routes):
    token_full = tokens.astype(jnp.float32)
    normed = rms_scale(token_full, attn_gain.astype(jnp.float32)).astype(jnp.bfloat16)
    projected = jnp.dot(normed, qkv_weight, preferred_element_type=jnp.float32).reshape(TOKENS, KV_HEADS, GROUP + 2, HEAD)
    places = (lengths[:, None] + jnp.arange(NEW, dtype=jnp.int32)[None, :]).reshape(TOKENS).astype(jnp.float32)
    queries = rotate(projected[:, :, :GROUP], places).astype(jnp.bfloat16)
    new_keys = rotate(projected[:, :, GROUP], places).astype(jnp.bfloat16)
    new_values = projected[:, :, GROUP + 1].astype(jnp.bfloat16)
    seen_all = visible(jnp.arange(CACHE, dtype=jnp.int32), lengths, WINDOW)
    causal = jnp.arange(NEW)[:, None] >= jnp.arange(NEW)[None, :]
    factor = 1.0 / HEAD ** 0.5

    def one_request(packed):
        query, key_new, value_new, key_old, value_old, seen = packed
        query_f = query.astype(jnp.float32)
        old_scores = jnp.einsum('tgqd,sgd->tgqs', query_f, key_old.reshape(CACHE, KV_HEADS, HEAD).astype(jnp.float32)) * factor
        new_scores = jnp.einsum('tgqd,ugd->tgqu', query_f, key_new.astype(jnp.float32)) * factor
        old_scores = jnp.where(seen[:, None, None, :], old_scores, -jnp.inf)
        new_scores = jnp.where(causal[:, None, None, :], new_scores, -jnp.inf)
        scores = jnp.concatenate([old_scores, new_scores], axis=-1)
        top_score = lax.optimization_barrier(jnp.max(scores, axis=-1, keepdims=True))
        weights = jnp.exp(scores - top_score)
        total = lax.optimization_barrier(jnp.sum(weights, axis=-1, keepdims=True))
        values_all = jnp.concatenate([value_old.reshape(CACHE, KV_HEADS, HEAD), value_new], axis=0).astype(jnp.float32)
        return jnp.einsum('tgqs,sgd->tgqd', weights, values_all) / total
    attended = lax.map(one_request, (queries.reshape(REQS, NEW, KV_HEADS, GROUP, HEAD), new_keys.reshape(REQS, NEW, KV_HEADS, HEAD), new_values.reshape(REQS, NEW, KV_HEADS, HEAD), cache_keys, cache_values, seen_all))
    attended = attended.reshape(TOKENS, HEADS * HEAD).astype(jnp.bfloat16)
    residual = token_full + jnp.dot(attended, out_weight, preferred_element_type=jnp.float32)
    scale = lax.rsqrt(lax.optimization_barrier(jnp.mean(residual * residual, axis=-1)) + EPSILON)
    gained = residual * moe_gain.astype(jnp.float32)
    logits = scale[:, None] * jnp.dot(gained, router_weight.astype(jnp.float32), precision=lax.Precision.HIGHEST)
    moe_in = (gained * scale[:, None]).astype(jnp.bfloat16)
    chosen = jnp.take_along_axis(logits, routes, axis=1)
    gate_prob = jax.nn.softmax(chosen, axis=-1)
    gate_all = jnp.einsum('td,edf->tef', moe_in.astype(jnp.float32), expert_gate.astype(jnp.float32))
    up_all = jnp.einsum('td,edf->tef', moe_in.astype(jnp.float32), expert_up.astype(jnp.float32))
    gate_pick = jnp.take_along_axis(gate_all, routes[:, :, None], axis=1)
    up_pick = jnp.take_along_axis(up_all, routes[:, :, None], axis=1)
    activated = (jax.nn.silu(gate_pick) * up_pick).astype(jnp.bfloat16)
    scaled = (gate_prob[:, :, None] * activated.astype(jnp.float32)).astype(jnp.bfloat16)
    onehot = (routes[:, :, None] == jnp.arange(EXPERTS, dtype=jnp.int32)[None, None, :]).astype(jnp.float32)
    spread = jnp.einsum('tke,tkf->tef', onehot, scaled.astype(jnp.float32))
    moe_out = jnp.einsum('tef,efd->td', spread, expert_down.astype(jnp.float32))
    return (residual + moe_out).astype(jnp.bfloat16)
```

```python
import functools

import jax
import jax.numpy as jnp
from jax import lax
from jax.experimental import pallas as pl
from jax.experimental.pallas import tpu as pltpu
from jax.sharding import Mesh, PartitionSpec as P

D = 1536
HEAD = 64
EXPERTS = 40
TOP = 8
SINK = 4
NEW = 4
GROUP = 3
REQS = 32
TOKENS = 128
WINDOW = 2044
SLOTS = 32
FEAT = 384
FF = 8

EPSILON = 1e-06
ROPE_BASE = 10000.0
FLOOR_SCORE = -1e30

F32 = jnp.float32
BF16 = jnp.bfloat16
VMEM = pl.BlockSpec(memory_space=pltpu.VMEM)
SMEM = pl.BlockSpec(memory_space=pltpu.SMEM)


def iota(shape, dim):
    return lax.broadcasted_iota(jnp.int32, shape, dim)


def dot(a, b):
    return jnp.dot(a, b, preferred_element_type=F32)


def dot_t(a, b):
    return lax.dot_general(a, b, (((1,), (1,)), ((), ())), preferred_element_type=F32)


def call(body, outs, n_in, smem=(), scratch=(), flops=10**7):
    return pl.pallas_call(
        body,
        out_shape=outs,
        in_specs=[SMEM if i in smem else VMEM for i in range(n_in)],
        out_specs=jax.tree.map(lambda _: VMEM, outs),
        scratch_shapes=list(scratch),
        cost_estimate=pl.CostEstimate(flops=flops, bytes_accessed=10**6, transcendentals=0),
    )


def attend_body(len_ref, tok_ref, gain_ref, w_ref, cos_ref, sin_ref, k_ref, v_ref, keep_ref, send_ref):
    core = lax.axis_index("core")
    seq = (lax.axis_index("z") * 4 + lax.axis_index("y")) * 2 + core
    x = tok_ref[...].astype(F32)
    normed = x * lax.rsqrt(jnp.mean(x * x, axis=-1, keepdims=True) + EPSILON) * gain_ref[...]
    proj = dot(normed.astype(BF16), w_ref[...])
    cos = cos_ref[...]
    sin = sin_ref[...]
    lane = iota((TOKENS, 128), 1)
    low = lane < 64
    first = (lane % 64) < 32
    tiles = [proj[:, 128 * i : 128 * i + 128] for i in range(5)]

    def rot(t):
        swapped = jnp.where(first, pltpu.roll(t, 96, 1), pltpu.roll(t, 32, 1))
        return t * cos + swapped * sin

    turned = [rot(t) for t in tiles]
    query = []
    for g in range(2):
        for q in range(GROUP):
            at = g * 5 + q
            t = turned[at // 2]
            if at % 2 != g:
                t = pltpu.roll(t, 64, 1)
            query.append(jnp.where(low if g == 0 else ~low, t * 0.125, 0.0).astype(BF16))
    key_new = jnp.where(low, pltpu.roll(turned[1], 64, 1), pltpu.roll(turned[4], 64, 1)).astype(BF16)
    value_new = jnp.where(low, tiles[2], tiles[4]).astype(BF16)

    row = iota((32, 256), 0)
    col = iota((32, 256), 1)
    same = (row // NEW) == (col // SLOTS)
    slot = seq * SLOTS + col % SLOTS
    nrow = iota((32, 32), 0)
    ncol = iota((32, 32), 1)
    ok_new = (nrow // NEW == ncol // NEW) & (ncol <= nrow) & (seq == 0)
    glow = iota((32, 128), 1) < 64
    glane = iota((32, 128), 1)
    for grp in range(4):
        lens = jnp.zeros((32, 256), jnp.int32)
        for r in range(8):
            lens = jnp.where(row // NEW == r, len_ref[grp * 8 + r], lens)
        back = lens - 1 - slot
        live = back >= 0
        safe = jnp.maximum(back, 0)
        age = safe - ((safe * 32833) >> 26) * WINDOW
        ok = same & live & ((slot < SINK) | (age <= WINDOW - 1 - row % NEW))
        rows = slice(grp * 32, grp * 32 + 32)
        qg = jnp.concatenate([b[rows] for b in query], axis=0)
        s = dot_t(qg, k_ref[grp * 256 : grp * 256 + 256, :]).reshape(6, 32, 256)
        sn = dot_t(qg, key_new[rows]).reshape(6, 32, 32)
        s = jnp.where(ok[None], s, FLOOR_SCORE)
        sn = jnp.where(ok_new[None], sn, FLOOR_SCORE)
        m = jnp.maximum(jnp.max(s, axis=-1, keepdims=True), jnp.max(sn, axis=-1, keepdims=True))
        p = jnp.where(ok[None], jnp.exp(s - m), 0.0)
        pn = jnp.where(ok_new[None], jnp.exp(sn - m), 0.0)
        mass = jnp.sum(p, axis=-1, keepdims=True) + jnp.sum(pn, axis=-1, keepdims=True)
        acc = dot(p.reshape(192, 256).astype(BF16), v_ref[grp * 256 : grp * 256 + 256, :]) + dot(
            pn.reshape(192, 32).astype(BF16), value_new[rows]
        )
        some = mass > 0.0
        mass = jnp.where(some, mass, 1.0)
        acc = acc.reshape(6, 32, 128) / mass
        lse = jnp.where(some, m + jnp.log(mass), FLOOR_SCORE)
        packed = []
        for g in range(2):
            a = [acc[g * 3 + q] for q in range(3)]
            a = [b if q % 2 == g else pltpu.roll(b, 64, 1) for q, b in enumerate(a)]
            e = [lse[g * 3 + q] for q in range(3)]
            stats = jnp.where(glane == 64, e[0], jnp.where(glane == 65, e[1], jnp.where(glane == 66, e[2], 0.0)))
            packed.append((jnp.where(glow, a[0], a[1]), jnp.where(glow, a[2], stats)))
        mine = core == 0
        for i in range(2):
            lanes = slice(128 * i, 128 * i + 128)
            keep_ref[rows, lanes] = jnp.where(mine, packed[0][i], packed[1][i])
            send_ref[rows, lanes] = jnp.where(mine, packed[1][i], packed[0][i])


def merge(parts):
    top = functools.reduce(jnp.maximum, [e for _, _, e in parts])
    weights = [jnp.exp(e - top) for _, _, e in parts]
    total = sum(weights)
    lo = hi = 0.0
    glow = iota(total.shape, 1) < 64
    for w, (a, b, _) in zip(weights, parts):
        w = w / total
        lo = lo + a * jnp.where(glow, w[:, 64:65], w[:, 65:66])
        hi = hi + b * w[:, 66:67]
    return lo, hi, top + jnp.log(total)


def encode(lo, hi, lse):
    lane = iota(lse.shape, 1)
    a = lse.astype(BF16).astype(F32)
    b = (lse - a).astype(BF16).astype(F32)
    c = lse - a - b
    tail = jnp.where(lane < 67, a, jnp.where(lane < 70, pltpu.roll(b, 3, 1), pltpu.roll(c, 6, 1)))
    tail = jnp.where(lane < 73, tail, 0.0)
    return lo.astype(BF16), jnp.where(lane < 64, hi, tail).astype(BF16)


def decode(block):
    lo = block[:, :128].astype(F32)
    hi = block[:, 128:].astype(F32)
    lse = hi + pltpu.roll(hi, 125, 1) + pltpu.roll(hi, 122, 1)
    lane = iota(lse.shape, 1)
    return lo, hi, jnp.where((lane >= 64) & (lane < 67), lse, 0.0)


def merge_core_body(keep_ref, got_ref, out_ref):
    lane = iota((TOKENS, 128), 1)
    parts = []
    for ref in (keep_ref, got_ref):
        hi = ref[:, 128:]
        parts.append((ref[:, :128], hi, jnp.where(lane >= 64, hi, 0.0)))
    lo, hi = encode(*merge(parts))
    out_ref[:, :128] = lo
    out_ref[:, 128:] = hi


def merge_y_body(in_ref, out_ref):
    lo, hi = encode(*merge([decode(in_ref[i]) for i in range(4)]))
    for i in range(8):
        out_ref[i, :, :128] = lo
        out_ref[i, :, 128:] = hi


def merge_z_body(in_ref, out_ref):
    lo, hi, _ = merge([decode(in_ref[i]) for i in range(8)])
    lo = lo.astype(BF16)
    hi = hi.astype(BF16)
    for i in range(16):
        out_ref[i, :, :128] = lo
        out_ref[i, :, 128:] = hi


def split3(v):
    a = v.astype(BF16)
    r = v - a.astype(F32)
    b = r.astype(BF16)
    return a, b, (r - b.astype(F32)).astype(BF16)


def project_body(mine_ref, other_ref, tok_ref, w_ref, gain_ref, router_ref, gate_ref, up_ref, routes_ref, res_ref, out_ref):
    core = lax.axis_index("core")
    tp = lax.axis_index("tp")
    acc = tok_ref[:, pl.ds(pl.multiple_of(tp * FEAT, 128), FEAT)].astype(F32)
    for ref, c in ((mine_ref, core), (other_ref, 1 - core)):
        for x in range(4):
            a = jnp.concatenate([ref[y * 4 + x] for y in range(4)], axis=0)[:, :192]
            at = pl.multiple_of((2 * x + c) * 192, 64)
            acc = acc + dot(a, w_ref[pl.ds(at, 192), :])
    res_ref[...] = acc
    gained = acc * gain_ref[...]
    squares = jnp.sum(acc * acc, axis=-1, keepdims=True)
    router = router_ref[...]
    g0, g1, g2 = split3(gained)
    logits = dot_t(g0, router) + dot_t(g1, router) + dot_t(g2, router)
    both = jnp.concatenate([dot_t(g0, gate_ref[...]), dot_t(g0, up_ref[...])], axis=1)
    routes = routes_ref[...]
    expert = (iota((TOKENS, 640), 1) % 320) // FF
    elane = iota((TOKENS, EXPERTS), 1)
    lane = iota((TOKENS, 128), 1)
    frow = iota((640, 128), 0)
    fcol = iota((640, 128), 1)
    fold = (frow % FF == fcol % FF) & (frow // 320 == fcol // 64)
    picks = jnp.zeros((TOKENS, 128), F32)
    stats = jnp.where(lane == TOP, squares, 0.0)
    for k in range(TOP):
        r = routes[:, k : k + 1]
        chosen = jnp.sum(jnp.where(elane == r, logits, 0.0), axis=-1, keepdims=True)
        stats = jnp.where(lane == k, chosen, stats)
        f = (fold & ((fcol % 64) // FF == k)).astype(BF16)
        picks = picks + dot(jnp.where(expert == r, both, 0.0).astype(BF16), f)
    a, b, c = (v.astype(F32) for v in split3(stats))
    tail = (a + pltpu.roll(b, 16, 1) + pltpu.roll(c, 32, 1)).astype(BF16)
    picks = picks.astype(BF16)
    for i in range(4):
        out_ref[i, :, :128] = picks
        out_ref[i, :, 128:] = tail


def expert_body(in_ref, routes_ref, down_ref, keep_ref, send_ref, part_ref):
    core = lax.axis_index("core")
    lane = iota((TOKENS, 128), 1)
    picks = sum(in_ref[i, :, :128].astype(F32) for i in range(4))
    tail = sum(in_ref[i, :, 128:].astype(F32) for i in range(4))
    stats = tail + pltpu.roll(tail, 112, 1) + pltpu.roll(tail, 96, 1)
    scale = lax.rsqrt(stats[:, TOP : TOP + 1] / D + EPSILON)
    logits = jnp.where(lane < TOP, stats * scale, FLOOR_SCORE)
    weights = jnp.exp(logits - jnp.max(logits, axis=-1, keepdims=True))
    prob = weights / jnp.sum(weights, axis=-1, keepdims=True)
    gate = picks * scale
    up = pltpu.roll(gate, 64, 1)
    activated = (gate / (1.0 + jnp.exp(-gate)) * up).astype(BF16).astype(F32)
    wide = jnp.zeros((TOKENS, 128), F32)
    for k in range(TOP):
        wide = jnp.where(lane // FF == k, prob[:, k : k + 1], wide)
    scaled = jnp.where(lane < 64, wide * activated, 0.0).astype(BF16)
    erow = iota((128, 1024), 0)
    ecol = iota((128, 1024), 1)
    spread_to = ((erow % FF == ecol % FF) & (erow // FF == ecol // 128)).astype(BF16)
    tiled = dot(scaled, spread_to)
    routes = routes_ref[...]
    spread = []
    for i in range(3):
        s = jnp.zeros((TOKENS, 128), F32)
        for k in range(TOP):
            s = jnp.where(lane // FF + 16 * i == routes[:, k : k + 1], tiled[:, 128 * k : 128 * k + 128], s)
        spread.append(s)
    spread = jnp.concatenate(spread, axis=1)[:, :320].astype(BF16)
    part_ref[...] = dot(spread, down_ref[...])
    keep_ref[...] = part_ref[pl.ds(pl.multiple_of(core * 64, 64), 64), :]
    send_ref[...] = part_ref[pl.ds(pl.multiple_of((1 - core) * 64, 64), 64), :]


def swap(v):
    return lax.ppermute(v, "core", [(0, 1), (1, 0)])


def exchange(v, axes):
    return lax.all_to_all(v, axes, 0, 0, tiled=True)


def on_device(
    tokens,
    attn_gain,
    qkv_weight,
    out_weight,
    moe_gain,
    router_weight,
    expert_gate,
    expert_up,
    expert_down,
    cache_keys,
    cache_values,
    lengths,
    routes,
):
    core = lax.axis_index("core")
    sds = jax.ShapeDtypeStruct
    places = (lengths[:, None] + jnp.arange(NEW, dtype=jnp.int32)[None, :]).reshape(TOKENS).astype(F32)
    half = HEAD // 2
    freqs = jnp.exp(-jnp.log(ROPE_BASE) * jnp.arange(half, dtype=F32) / half)
    angles = places[:, None] * jnp.tile(freqs, 4)[None, :]
    cos = jnp.cos(angles)
    sin = jnp.where(jnp.arange(128)[None, :] % 64 < half, -jnp.sin(angles), jnp.sin(angles))

    keep, send = call(attend_body, (sds((TOKENS, 256), F32),) * 2, 8, smem=(0,))(
        lengths,
        tokens,
        attn_gain.reshape(1, D),
        qkv_weight,
        cos,
        sin,
        cache_keys.reshape(REQS * SLOTS, 128),
        cache_values.reshape(REQS * SLOTS, 128),
    )
    packed = call(merge_core_body, sds((TOKENS, 256), BF16), 2)(keep, swap(send))
    packed = exchange(packed.reshape(4, 32, 256), "y")
    packed = call(merge_y_body, sds((8, 32, 256), BF16), 1)(packed)
    packed = exchange(packed, "z")
    packed = call(merge_z_body, sds((16, 32, 256), BF16), 1)(packed)
    mine = exchange(packed, ("y", "tp"))
    other = swap(mine)

    residual, picked = call(project_body, (sds((TOKENS, FEAT), F32), sds((4, TOKENS, 256), BF16)), 9)(
        mine,
        other,
        tokens,
        out_weight,
        moe_gain.reshape(1, FEAT),
        router_weight.T,
        expert_gate.transpose(0, 2, 1).reshape(EXPERTS * FF, FEAT),
        expert_up.transpose(0, 2, 1).reshape(EXPERTS * FF, FEAT),
        routes,
    )
    picked = exchange(picked, "tp")
    keep, send = call(
        expert_body,
        (sds((TOKENS // 2, FEAT), F32),) * 2,
        3,
        scratch=[pltpu.VMEM((TOKENS, FEAT), F32)],
    )(picked, routes, expert_down.reshape(EXPERTS * FF, FEAT))

    part = (keep + swap(send)).astype(BF16)
    part = exchange(jnp.broadcast_to(part, (4,) + part.shape), "y")
    part = jnp.sum(part.astype(F32), axis=0).astype(BF16)
    part = exchange(jnp.broadcast_to(part, (8,) + part.shape), "z")
    own = lax.dynamic_slice_in_dim(residual, core * (TOKENS // 2), TOKENS // 2, 0)
    own = (own + jnp.sum(part.astype(F32), axis=0)).astype(BF16)
    theirs = swap(own)
    first = core == 0
    return jnp.concatenate([jnp.where(first, own, theirs), jnp.where(first, theirs, own)], axis=0)


def solution(mesh):
    seq = ("z", "y", "core")
    grid = Mesh(mesh.devices.reshape(8, 4, 2, 4), seq + ("tp",))
    in_specs = (
        P(),
        P(),
        P(None, "tp"),
        P(None, "tp"),
        P("tp"),
        P("tp", None),
        P(None, "tp", seq),
        P(None, "tp", seq),
        P(None, seq, "tp"),
        P(None, seq, "tp"),
        P(None, seq, "tp"),
        P(),
        P(),
    )
    out_specs = P(None, "tp")
    return jax.shard_map(on_device, mesh=grid, in_specs=in_specs, out_specs=out_specs, check_vma=False)
```

```python
import functools

import jax
import jax.numpy as jnp
import numpy as np
from jax import lax
from jax.experimental import pallas as pl
from jax.experimental.pallas import tpu as pltpu
from jax.sharding import Mesh, PartitionSpec as P

D = 1536
HEAD = 64
EXPERTS = 40
TOP = 8
SINK = 4
NEW = 4
GROUP = 3
REQS = 32
TOKENS = 128
WINDOW = 2044
SLOTS = 32
FEAT = 384
FF = 8

EPSILON = 1e-06
ROPE_BASE = 10000.0
FLOOR_SCORE = -1e30

F32 = jnp.float32
BF16 = jnp.bfloat16
VMEM = pl.BlockSpec(memory_space=pltpu.VMEM)
SMEM = pl.BlockSpec(memory_space=pltpu.SMEM)


def iota(shape, dim):
    return lax.broadcasted_iota(jnp.int32, shape, dim)


def dot(a, b):
    return jnp.dot(a, b, preferred_element_type=F32)


def dot_t(a, b):
    return lax.dot_general(a, b, (((1,), (1,)), ((), ())), preferred_element_type=F32)


def call(body, outs, args, smem=(), scratch=(), flops=10**7):
    outs = [pltpu.VMEM(shape, dtype) for shape, dtype in outs]
    run = pl.pallas_call(
        body,
        out_shape=outs,
        in_specs=[SMEM if i in smem else VMEM for i in range(len(args))],
        out_specs=[VMEM for _ in outs],
        scratch_shapes=list(scratch),
        cost_estimate=pl.CostEstimate(flops=flops, bytes_accessed=10**6, transcendentals=0),
    )
    space = [pltpu.MemorySpace.SMEM if i in smem else pltpu.MemorySpace.VMEM for i in range(len(args))]
    return run(*[pltpu.with_memory_space_constraint(a, m) for a, m in zip(args, space)])


def cos_sin(angle):
    turns = jnp.floor(angle * (2.0 / np.pi) + 0.5)
    r = angle - turns * QUARTER[0]
    r = r - turns * QUARTER[1]
    r = r - turns * QUARTER[2]
    r = r - turns * QUARTER[3]
    r2 = r * r
    sin = r + r * r2 * (-1.0 / 6 + r2 * (1.0 / 120 + r2 * (-1.0 / 5040 + r2 * (1.0 / 362880))))
    cos = 1.0 - 0.5 * r2 + r2 * r2 * (1.0 / 24 + r2 * (-1.0 / 720 + r2 * (1.0 / 40320 - r2 * (1.0 / 3628800))))
    which = turns.astype(jnp.int32) & 3
    odd = (which & 1) == 1
    c = jnp.where(odd, sin, cos)
    s = jnp.where(odd, cos, sin)
    return jnp.where((which == 1) | (which == 2), -c, c), jnp.where(which >= 2, -s, s)


def quarter_pieces():
    pieces = []
    rest = np.pi / 2
    for _ in range(3):
        top = np.floor(rest * 2.0 ** (7 - np.floor(np.log2(rest)))) / 2.0 ** (7 - np.floor(np.log2(rest)))
        pieces.append(float(top))
        rest = rest - top
    return pieces + [float(np.float32(rest))]


QUARTER = quarter_pieces()


def attend_body(len_ref, tok_ref, gain_ref, w_ref, freq_ref, k_ref, v_ref, out_ref):
    seq = ((lax.axis_index("zh") * 2 + lax.axis_index("zl")) * 4 + lax.axis_index("y")) * 2 + lax.axis_index("core")
    x = tok_ref[...].astype(F32)
    normed = x * lax.rsqrt(jnp.mean(x * x, axis=-1, keepdims=True) + EPSILON) * gain_ref[...]
    proj = dot(normed.astype(BF16), w_ref[...])
    lane = iota((32, 128), 1)
    row = iota((32, 128), 0)
    low = lane < 64
    first = (lane % 64) < 32
    slot = seq * SLOTS + lane % SLOTS
    nrow = iota((32, 32), 0)
    ncol = iota((32, 32), 1)
    ok_new = (nrow // NEW == ncol // NEW) & (ncol <= nrow) & (seq == 0)
    freq = freq_ref[...]
    for grp in range(4):
        rows = slice(grp * 32, grp * 32 + 32)
        lens = jnp.zeros((32, 128), jnp.int32)
        for r in range(8):
            lens = jnp.where(row // NEW == r, len_ref[grp * 8 + r], lens)
        cos, sin = cos_sin((lens + row % NEW).astype(F32) * freq)
        sin = jnp.where(first, -sin, sin)
        tiles = [proj[rows, 128 * i : 128 * i + 128] for i in range(5)]
        turned = [t * cos + jnp.where(first, pltpu.roll(t, 96, 1), pltpu.roll(t, 32, 1)) * sin for t in tiles]
        query = []
        for g in range(2):
            for q in range(GROUP):
                at = g * 5 + q
                t = turned[at // 2]
                if at % 2 != g:
                    t = pltpu.roll(t, 64, 1)
                query.append(jnp.where(low if g == 0 else ~low, t * 0.125, 0.0).astype(BF16))
        qg = jnp.concatenate(query, axis=0)
        key_new = jnp.where(low, pltpu.roll(turned[1], 64, 1), pltpu.roll(turned[4], 64, 1)).astype(BF16)
        value_new = jnp.where(low, tiles[2], tiles[4]).astype(BF16)

        back = lens - 1 - slot
        safe = jnp.maximum(back, 0)
        age = safe - ((safe * 32833) >> 26) * WINDOW
        ok = (back >= 0) & ((slot < SINK) | (age <= WINDOW - 1 - row % NEW))
        ok = jnp.concatenate([ok & (row // NEW == lane // SLOTS + 4 * i) for i in range(2)], axis=1)
        s = dot_t(qg, k_ref[grp * 256 : grp * 256 + 256, :]).reshape(6, 32, 256)
        sn = dot_t(qg, key_new).reshape(6, 32, 32)
        s = jnp.where(ok[None], s, FLOOR_SCORE)
        sn = jnp.where(ok_new[None], sn, FLOOR_SCORE)
        m = jnp.maximum(jnp.max(s, axis=-1, keepdims=True), jnp.max(sn, axis=-1, keepdims=True))
        p = jnp.where(ok[None], jnp.exp(s - m), 0.0)
        pn = jnp.where(ok_new[None], jnp.exp(sn - m), 0.0)
        mass = jnp.sum(p, axis=-1, keepdims=True) + jnp.sum(pn, axis=-1, keepdims=True)
        acc = dot(p.reshape(192, 256).astype(BF16), v_ref[grp * 256 : grp * 256 + 256, :]) + dot(
            pn.reshape(192, 32).astype(BF16), value_new
        )
        some = mass > 0.0
        mass = jnp.where(some, mass, 1.0)
        acc = acc.reshape(6, 32, 128) / mass
        lse = jnp.where(some, m + jnp.log(mass), FLOOR_SCORE)
        for g in range(2):
            a = [acc[g * 3 + q] for q in range(3)]
            a = [b if q % 2 == g else pltpu.roll(b, 64, 1) for q, b in enumerate(a)]
            e = [lse[g * 3 + q] for q in range(3)]
            stats = jnp.where(lane == 64, e[0], jnp.where(lane == 65, e[1], jnp.where(lane == 66, e[2], 0.0)))
            lo, hi = encode(jnp.where(low, a[0], a[1]), a[2], stats)
            out_ref[grp * 2 + g, :, :128] = lo
            out_ref[grp * 2 + g, :, 128:] = hi


def merge(parts):
    top = functools.reduce(jnp.maximum, [e for _, _, e in parts])
    weights = [jnp.exp(e - top) for _, _, e in parts]
    total = sum(weights)
    lo = hi = 0.0
    glow = iota(total.shape, 1) < 64
    for w, (a, b, _) in zip(weights, parts):
        w = w / total
        lo = lo + a * jnp.where(glow, w[:, 64:65], w[:, 65:66])
        hi = hi + b * w[:, 66:67]
    return lo, hi, top + jnp.log(total)


def encode(lo, hi, lse):
    lane = iota(lse.shape, 1)
    a = lse.astype(BF16).astype(F32)
    b = (lse - a).astype(BF16).astype(F32)
    c = lse - a - b
    tail = jnp.where(lane < 67, a, jnp.where(lane < 70, pltpu.roll(b, 3, 1), pltpu.roll(c, 6, 1)))
    tail = jnp.where(lane < 73, tail, 0.0)
    return lo.astype(BF16), jnp.where(lane < 64, hi, tail).astype(BF16)


def decode(block):
    lo = block[:, :128].astype(F32)
    hi = block[:, 128:].astype(F32)
    lse = hi + pltpu.roll(hi, 125, 1) + pltpu.roll(hi, 122, 1)
    lane = iota(lse.shape, 1)
    return lo, hi, jnp.where((lane >= 64) & (lane < 67), lse, 0.0)


def merge_y_body(in_ref, out_ref):
    lo, hi = encode(*merge([decode(in_ref[i]) for i in range(8)]))
    for i in range(8):
        out_ref[i, :, :128] = lo
        out_ref[i, :, 128:] = hi


def merge_z_body(in_ref, out_ref):
    lo, hi, _ = merge([decode(in_ref[i]) for i in range(8)])
    lo = lo.astype(BF16)
    hi = hi.astype(BF16)
    for i in range(16):
        out_ref[i, :, :128] = lo
        out_ref[i, :, 128:] = hi


def split3(v):
    a = v.astype(BF16)
    r = v - a.astype(F32)
    b = r.astype(BF16)
    return a, b, (r - b.astype(F32)).astype(BF16)


def project_body(mine_ref, other_ref, tok_ref, w_ref, gain_ref, router_ref, gate_ref, up_ref, routes_ref, res_ref, out_ref):
    core = lax.axis_index("core")
    tp = lax.axis_index("tp")
    acc = tok_ref[:, pl.ds(pl.multiple_of(tp * FEAT, 128), FEAT)].astype(F32)
    for ref, c in ((mine_ref, core), (other_ref, 1 - core)):
        for x in range(4):
            a = jnp.concatenate([ref[y * 4 + x] for y in range(4)], axis=0)[:, :192]
            at = pl.multiple_of((2 * x + c) * 192, 64)
            acc = acc + dot(a, w_ref[pl.ds(at, 192), :])
    res_ref[...] = acc
    gained = acc * gain_ref[...]
    squares = jnp.sum(acc * acc, axis=-1, keepdims=True)
    router = router_ref[...]
    g0, g1, g2 = split3(gained)
    logits = dot_t(g0, router) + dot_t(g1, router) + dot_t(g2, router)
    both = jnp.concatenate([dot_t(g0, gate_ref[...]), dot_t(g0, up_ref[...])], axis=1)
    routes = routes_ref[...].T
    expert = (iota((TOKENS, 640), 1) % 320) // FF
    elane = iota((TOKENS, EXPERTS), 1)
    lane = iota((TOKENS, 128), 1)
    frow = iota((640, 128), 0)
    fcol = iota((640, 128), 1)
    fold = (frow % FF == fcol % FF) & (frow // 320 == fcol // 64)
    picks = jnp.zeros((TOKENS, 128), F32)
    stats = jnp.where(lane == TOP, squares, 0.0)
    for k in range(TOP):
        r = routes[:, k : k + 1]
        chosen = jnp.sum(jnp.where(elane == r, logits, 0.0), axis=-1, keepdims=True)
        stats = jnp.where(lane == k, chosen, stats)
        f = (fold & ((fcol % 64) // FF == k)).astype(BF16)
        picks = picks + dot(jnp.where(expert == r, both, 0.0).astype(BF16), f)
    a, b, c = (v.astype(F32) for v in split3(stats))
    tail = (a + pltpu.roll(b, 16, 1) + pltpu.roll(c, 32, 1)).astype(BF16)
    picks = picks.astype(BF16)
    for i in range(4):
        out_ref[i, :, :128] = picks
        out_ref[i, :, 128:] = tail


def expert_body(in_ref, routes_ref, down_ref, keep_ref, send_ref, part_ref):
    core = lax.axis_index("core")
    lane = iota((TOKENS, 128), 1)
    picks = sum(in_ref[i, :, :128].astype(F32) for i in range(4))
    tail = sum(in_ref[i, :, 128:].astype(F32) for i in range(4))
    stats = tail + pltpu.roll(tail, 112, 1) + pltpu.roll(tail, 96, 1)
    scale = lax.rsqrt(stats[:, TOP : TOP + 1] / D + EPSILON)
    logits = jnp.where(lane < TOP, stats * scale, FLOOR_SCORE)
    weights = jnp.exp(logits - jnp.max(logits, axis=-1, keepdims=True))
    prob = weights / jnp.sum(weights, axis=-1, keepdims=True)
    gate = picks * scale
    up = pltpu.roll(gate, 64, 1)
    activated = (gate / (1.0 + jnp.exp(-gate)) * up).astype(BF16).astype(F32)
    wide = jnp.zeros((TOKENS, 128), F32)
    for k in range(TOP):
        wide = jnp.where(lane // FF == k, prob[:, k : k + 1], wide)
    scaled = jnp.where(lane < 64, wide * activated, 0.0).astype(BF16)
    erow = iota((128, 1024), 0)
    ecol = iota((128, 1024), 1)
    spread_to = ((erow % FF == ecol % FF) & (erow // FF == ecol // 128)).astype(BF16)
    tiled = dot(scaled, spread_to)
    routes = routes_ref[...].T
    spread = []
    for i in range(3):
        s = jnp.zeros((TOKENS, 128), F32)
        for k in range(TOP):
            s = jnp.where(lane // FF + 16 * i == routes[:, k : k + 1], tiled[:, 128 * k : 128 * k + 128], s)
        spread.append(s)
    spread = jnp.concatenate(spread, axis=1)[:, :320].astype(BF16)
    part_ref[...] = dot(spread, down_ref[...])
    keep_ref[...] = part_ref[pl.ds(pl.multiple_of(core * 64, 64), 64), :]
    send_ref[...] = part_ref[pl.ds(pl.multiple_of((1 - core) * 64, 64), 64), :]


def swap(v):
    return lax.ppermute(v, "core", [(0, 1), (1, 0)])


def exchange(v, axes):
    return lax.all_to_all(v, axes, 0, 0, tiled=True)


def on_device(
    tokens,
    attn_gain,
    qkv_weight,
    out_weight,
    moe_gain,
    router_weight,
    expert_gate,
    expert_up,
    expert_down,
    cache_keys,
    cache_values,
    lengths,
    routes,
):
    core = lax.axis_index("core")
    z = ("zh", "zl")
    half = HEAD // 2
    freqs = np.tile(np.exp(-np.log(ROPE_BASE) * np.arange(half) / half), 4).astype(np.float32)
    (packed,) = call(
        attend_body,
        [((8, 32, 256), BF16)],
        (
            lengths,
            tokens,
            attn_gain.reshape(1, D),
            qkv_weight,
            jnp.asarray(freqs[None, :]),
            cache_keys.reshape(REQS * SLOTS, 128),
            cache_values.reshape(REQS * SLOTS, 128),
        ),
        smem=(0,),
    )
    (packed,) = call(merge_y_body, [((8, 32, 256), BF16)], (exchange(packed, ("y", "core")),))
    (packed,) = call(merge_z_body, [((16, 32, 256), BF16)], (exchange(packed, z),))
    mine = exchange(packed, ("y", "tp"))
    other = swap(mine)

    residual, picked = call(
        project_body,
        [((TOKENS, FEAT), F32), ((4, TOKENS, 256), BF16)],
        (
            mine,
            other,
            tokens,
            out_weight,
            moe_gain.reshape(1, FEAT),
            router_weight.T,
            expert_gate.transpose(0, 2, 1).reshape(EXPERTS * FF, FEAT),
            expert_up.transpose(0, 2, 1).reshape(EXPERTS * FF, FEAT),
            routes.T,
        ),
    )
    keep, send = call(
        expert_body,
        [((TOKENS // 2, FEAT), F32)] * 2,
        (exchange(picked, "tp"), routes.T, expert_down.reshape(EXPERTS * FF, FEAT)),
        scratch=[pltpu.VMEM((TOKENS, FEAT), F32)],
    )

    part = (keep + swap(send)).astype(BF16)
    part = exchange(jnp.broadcast_to(part, (8,) + part.shape), ("zl", "y"))
    part = jnp.sum(part.astype(F32), axis=0).astype(BF16)
    part = exchange(jnp.broadcast_to(part, (4,) + part.shape), "zh")
    own = lax.dynamic_slice_in_dim(residual, core * (TOKENS // 2), TOKENS // 2, 0)
    own = (own + jnp.sum(part.astype(F32), axis=0)).astype(BF16)
    theirs = swap(own)
    first = core == 0
    return jnp.concatenate([jnp.where(first, own, theirs), jnp.where(first, theirs, own)], axis=0)


def solution(mesh):
    seq = ("zh", "zl", "y", "core")
    grid = Mesh(mesh.devices.reshape(4, 2, 4, 2, 4), seq + ("tp",))
    in_specs = (
        P(),
        P(),
        P(None, "tp"),
        P(None, "tp"),
        P("tp"),
        P("tp", None),
        P(None, "tp", seq),
        P(None, "tp", seq),
        P(None, seq, "tp"),
        P(None, seq, "tp"),
        P(None, seq, "tp"),
        P(),
        P(),
    )
    out_specs = P(None, "tp")
    return jax.shard_map(on_device, mesh=grid, in_specs=in_specs, out_specs=out_specs, check_vma=False)
```

```python
import functools

import jax
import jax.numpy as jnp
import numpy as np
from jax import lax
from jax.experimental import pallas as pl
from jax.experimental.pallas import tpu as pltpu
from jax.sharding import Mesh, PartitionSpec as P

D = 1536
HEAD = 64
EXPERTS = 40
TOP = 8
SINK = 4
NEW = 4
GROUP = 3
REQS = 32
TOKENS = 128
WINDOW = 2044
SLOTS = 32
FEAT = 384
FF = 8
CHUNKS = 4

EPSILON = 1e-06
ROPE_BASE = 10000.0
FLOOR_SCORE = -1e30

F32 = jnp.float32
BF16 = jnp.bfloat16
VMEM = pl.BlockSpec(memory_space=pltpu.VMEM)
SMEM = pl.BlockSpec(memory_space=pltpu.SMEM)


def iota(shape, dim):
    return lax.broadcasted_iota(jnp.int32, shape, dim)


def dot(a, b):
    return jnp.dot(a, b, preferred_element_type=F32)


def dot_t(a, b):
    return lax.dot_general(a, b, (((1,), (1,)), ((), ())), preferred_element_type=F32)


def call(body, outs, args, smem=(), raw=(), scratch=(), pinned=True):
    kinds = ["s" if i in smem else "r" if i in raw else "v" for i in range(len(args))]
    run = pl.pallas_call(
        body,
        out_shape=[(pltpu.VMEM if pinned else jax.ShapeDtypeStruct)(shape, dtype) for shape, dtype in outs],
        in_specs=[{"s": SMEM, "r": pl.BlockSpec(memory_space=pl.ANY), "v": VMEM}[k] for k in kinds],
        out_specs=[VMEM for _ in outs],
        scratch_shapes=list(scratch),
        cost_estimate=pl.CostEstimate(flops=10**7, bytes_accessed=10**6, transcendentals=0),
    )
    space = {"s": pltpu.MemorySpace.SMEM, "r": pl.ANY, "v": pltpu.MemorySpace.VMEM}
    return run(*[pltpu.with_memory_space_constraint(a, space[k]) for a, k in zip(args, kinds)])


def started(pairs, sems):
    copies = [pltpu.make_async_copy(src, dst, sems.at[i]) for i, (src, dst) in enumerate(pairs)]
    for c in copies:
        c.start()
    return copies


def cos_sin(angle):
    turns = jnp.floor(angle * (2.0 / np.pi) + 0.5)
    r = angle - turns * QUARTER[0]
    r = r - turns * QUARTER[1]
    r = r - turns * QUARTER[2]
    r = r - turns * QUARTER[3]
    r2 = r * r
    sin = r + r * r2 * (-1.0 / 6 + r2 * (1.0 / 120 + r2 * (-1.0 / 5040 + r2 * (1.0 / 362880))))
    cos = 1.0 - 0.5 * r2 + r2 * r2 * (1.0 / 24 + r2 * (-1.0 / 720 + r2 * (1.0 / 40320 - r2 * (1.0 / 3628800))))
    which = turns.astype(jnp.int32) & 3
    odd = (which & 1) == 1
    c = jnp.where(odd, sin, cos)
    s = jnp.where(odd, cos, sin)
    return jnp.where((which == 1) | (which == 2), -c, c), jnp.where(which >= 2, -s, s)


def quarter_pieces():
    pieces = []
    rest = np.pi / 2
    for _ in range(3):
        top = np.floor(rest * 2.0 ** (7 - np.floor(np.log2(rest)))) / 2.0 ** (7 - np.floor(np.log2(rest)))
        pieces.append(float(top))
        rest = rest - top
    return pieces + [float(np.float32(rest))]


QUARTER = quarter_pieces()


def attend_body(
    len_ref,
    tok_hbm,
    gain_hbm,
    w_hbm,
    k_hbm,
    v_hbm,
    out_ref,
    tok_ref,
    gain_ref,
    w_ref,
    k_ref,
    v_ref,
    sems,
):
    part = D // CHUNKS
    pairs = [(tok_hbm, tok_ref), (gain_hbm, gain_ref)]
    pairs += [(w_hbm.at[pl.ds(i * part, part)], w_ref.at[pl.ds(i * part, part)]) for i in range(CHUNKS)]
    pairs += [(k_hbm, k_ref), (v_hbm, v_ref)]
    copies = started(pairs, sems)
    seq = ((lax.axis_index("zh") * 2 + lax.axis_index("zl")) * 4 + lax.axis_index("y")) * 2 + lax.axis_index("core")
    half = HEAD // 2
    spot = iota((8, 128), 1) % half
    freq = jnp.zeros((8, 128), F32)
    for i in range(half):
        freq = jnp.where(spot == i, float(np.float32(ROPE_BASE ** (-i / half))), freq)
    freq = freq[:1]
    copies[0].wait()
    copies[1].wait()
    x = tok_ref[...].astype(F32)
    normed = x * lax.rsqrt(jnp.mean(x * x, axis=-1, keepdims=True) + EPSILON) * gain_ref[...].reshape(1, D)
    normed = normed.astype(BF16)
    proj = jnp.zeros((TOKENS, 640), F32)
    for i in range(CHUNKS):
        copies[2 + i].wait()
        proj = proj + dot(normed[:, i * part : (i + 1) * part], w_ref[i * part : (i + 1) * part, :])
    copies[2 + CHUNKS].wait()
    copies[3 + CHUNKS].wait()
    lane = iota((32, 128), 1)
    row = iota((32, 128), 0)
    low = lane < 64
    first = (lane % 64) < 32
    slot = seq * SLOTS + lane % SLOTS
    nrow = iota((32, 32), 0)
    ncol = iota((32, 32), 1)
    ok_new = (nrow // NEW == ncol // NEW) & (ncol <= nrow) & (seq == 0)
    for grp in range(4):
        rows = slice(grp * 32, grp * 32 + 32)
        lens = jnp.zeros((32, 128), jnp.int32)
        for r in range(8):
            lens = jnp.where(row // NEW == r, len_ref[grp * 8 + r], lens)
        cos, sin = cos_sin((lens + row % NEW).astype(F32) * freq)
        sin = jnp.where(first, -sin, sin)
        tiles = [proj[rows, 128 * i : 128 * i + 128] for i in range(5)]
        turned = [t * cos + jnp.where(first, pltpu.roll(t, 96, 1), pltpu.roll(t, 32, 1)) * sin for t in tiles]
        query = []
        for g in range(2):
            for q in range(GROUP):
                at = g * 5 + q
                t = turned[at // 2]
                if at % 2 != g:
                    t = pltpu.roll(t, 64, 1)
                query.append(jnp.where(low if g == 0 else ~low, t * 0.125, 0.0).astype(BF16))
        qg = jnp.concatenate(query, axis=0)
        key_new = jnp.where(low, pltpu.roll(turned[1], 64, 1), pltpu.roll(turned[4], 64, 1)).astype(BF16)
        value_new = jnp.where(low, tiles[2], tiles[4]).astype(BF16)

        back = lens - 1 - slot
        safe = jnp.maximum(back, 0)
        age = safe - ((safe * 32833) >> 26) * WINDOW
        ok = (back >= 0) & ((slot < SINK) | (age <= WINDOW - 1 - row % NEW))
        ok = jnp.concatenate([ok & (row // NEW == lane // SLOTS + 4 * i) for i in range(2)], axis=1)
        s = dot_t(qg, k_ref[grp * 256 : grp * 256 + 256, :]).reshape(6, 32, 256)
        sn = dot_t(qg, key_new).reshape(6, 32, 32)
        s = jnp.where(ok[None], s, FLOOR_SCORE)
        sn = jnp.where(ok_new[None], sn, FLOOR_SCORE)
        m = jnp.maximum(jnp.max(s, axis=-1, keepdims=True), jnp.max(sn, axis=-1, keepdims=True))
        p = jnp.where(ok[None], jnp.exp(s - m), 0.0)
        pn = jnp.where(ok_new[None], jnp.exp(sn - m), 0.0)
        mass = jnp.sum(p, axis=-1, keepdims=True) + jnp.sum(pn, axis=-1, keepdims=True)
        acc = dot(p.reshape(192, 256).astype(BF16), v_ref[grp * 256 : grp * 256 + 256, :]) + dot(
            pn.reshape(192, 32).astype(BF16), value_new
        )
        some = mass > 0.0
        mass = jnp.where(some, mass, 1.0)
        acc = acc.reshape(6, 32, 128) / mass
        lse = jnp.where(some, m + jnp.log(mass), FLOOR_SCORE)
        for g in range(2):
            a = [acc[g * 3 + q] for q in range(3)]
            a = [b if q % 2 == g else pltpu.roll(b, 64, 1) for q, b in enumerate(a)]
            e = [lse[g * 3 + q] for q in range(3)]
            stats = jnp.where(lane == 64, e[0], jnp.where(lane == 65, e[1], jnp.where(lane == 66, e[2], 0.0)))
            lo, hi = encode(jnp.where(low, a[0], a[1]), a[2], stats)
            out_ref[grp * 2 + g, :, :128] = lo
            out_ref[grp * 2 + g, :, 128:] = hi


def merge(parts):
    top = functools.reduce(jnp.maximum, [e for _, _, e in parts])
    weights = [jnp.exp(e - top) for _, _, e in parts]
    total = sum(weights)
    lo = hi = 0.0
    glow = iota(total.shape, 1) < 64
    for w, (a, b, _) in zip(weights, parts):
        w = w / total
        lo = lo + a * jnp.where(glow, w[:, 64:65], w[:, 65:66])
        hi = hi + b * w[:, 66:67]
    return lo, hi, top + jnp.log(total)


def encode(lo, hi, lse):
    lane = iota(lse.shape, 1)
    a = lse.astype(BF16).astype(F32)
    b = (lse - a).astype(BF16).astype(F32)
    c = lse - a - b
    tail = jnp.where(lane < 67, a, jnp.where(lane < 70, pltpu.roll(b, 3, 1), pltpu.roll(c, 6, 1)))
    tail = jnp.where(lane < 73, tail, 0.0)
    return lo.astype(BF16), jnp.where(lane < 64, hi, tail).astype(BF16)


def decode(block):
    lo = block[:, :128].astype(F32)
    hi = block[:, 128:].astype(F32)
    lse = hi + pltpu.roll(hi, 125, 1) + pltpu.roll(hi, 122, 1)
    lane = iota(lse.shape, 1)
    return lo, hi, jnp.where((lane >= 64) & (lane < 67), lse, 0.0)


def merge_y_body(in_ref, out_ref):
    lo, hi = encode(*merge([decode(in_ref[i]) for i in range(8)]))
    for i in range(8):
        out_ref[i, :, :128] = lo
        out_ref[i, :, 128:] = hi


def merge_z_body(in_ref, out_ref):
    lo, hi, _ = merge([decode(in_ref[i]) for i in range(8)])
    lo = lo.astype(BF16)
    hi = hi.astype(BF16)
    for i in range(16):
        out_ref[i, :, :128] = lo
        out_ref[i, :, 128:] = hi


def split3(v):
    a = v.astype(BF16)
    r = v - a.astype(F32)
    b = r.astype(BF16)
    return a, b, (r - b.astype(F32)).astype(BF16)


def project_body(
    mine_ref,
    other_ref,
    tok_ref,
    w_ref,
    gain_ref,
    router_ref,
    gate_hbm,
    up_hbm,
    routes_ref,
    res_ref,
    out_ref,
    gate_ref,
    up_ref,
    sems,
):
    copies = started([(gate_hbm, gate_ref), (up_hbm, up_ref)], sems)
    core = lax.axis_index("core")
    tp = lax.axis_index("tp")
    acc = tok_ref[:, pl.ds(pl.multiple_of(tp * FEAT, 128), FEAT)].astype(F32)
    for ref, c in ((mine_ref, core), (other_ref, 1 - core)):
        for x in range(4):
            a = jnp.concatenate([ref[y * 4 + x] for y in range(4)], axis=0)[:, :192]
            at = pl.multiple_of((2 * x + c) * 192, 64)
            acc = acc + dot(a, w_ref[pl.ds(at, 192), :])
    res_ref[...] = acc
    gained = acc * gain_ref[...]
    squares = jnp.sum(acc * acc, axis=-1, keepdims=True)
    router = router_ref[...]
    g0, g1, g2 = split3(gained)
    logits = dot_t(g0, router) + dot_t(g1, router) + dot_t(g2, router)
    for c in copies:
        c.wait()
    both = jnp.concatenate([dot_t(g0, gate_ref[...]), dot_t(g0, up_ref[...])], axis=1)
    routes = routes_ref[...].T
    expert = (iota((TOKENS, 640), 1) % 320) // FF
    elane = iota((TOKENS, EXPERTS), 1)
    lane = iota((TOKENS, 128), 1)
    frow = iota((640, 128), 0)
    fcol = iota((640, 128), 1)
    fold = (frow % FF == fcol % FF) & (frow // 320 == fcol // 64)
    picks = jnp.zeros((TOKENS, 128), F32)
    stats = jnp.where(lane == TOP, squares, 0.0)
    for k in range(TOP):
        r = routes[:, k : k + 1]
        chosen = jnp.sum(jnp.where(elane == r, logits, 0.0), axis=-1, keepdims=True)
        stats = jnp.where(lane == k, chosen, stats)
        f = (fold & ((fcol % 64) // FF == k)).astype(BF16)
        picks = picks + dot(jnp.where(expert == r, both, 0.0).astype(BF16), f)
    a, b, c = (v.astype(F32) for v in split3(stats))
    tail = (a + pltpu.roll(b, 16, 1) + pltpu.roll(c, 32, 1)).astype(BF16)
    picks = picks.astype(BF16)
    for i in range(4):
        out_ref[i, :, :128] = picks
        out_ref[i, :, 128:] = tail


def expert_body(in_ref, routes_ref, down_hbm, keep_ref, send_ref, part_ref, down_ref, sems):
    copies = started([(down_hbm, down_ref)], sems)
    core = lax.axis_index("core")
    lane = iota((TOKENS, 128), 1)
    picks = sum(in_ref[i, :, :128].astype(F32) for i in range(4))
    tail = sum(in_ref[i, :, 128:].astype(F32) for i in range(4))
    stats = tail + pltpu.roll(tail, 112, 1) + pltpu.roll(tail, 96, 1)
    scale = lax.rsqrt(stats[:, TOP : TOP + 1] / D + EPSILON)
    logits = jnp.where(lane < TOP, stats * scale, FLOOR_SCORE)
    weights = jnp.exp(logits - jnp.max(logits, axis=-1, keepdims=True))
    prob = weights / jnp.sum(weights, axis=-1, keepdims=True)
    gate = picks * scale
    up = pltpu.roll(gate, 64, 1)
    activated = (gate / (1.0 + jnp.exp(-gate)) * up).astype(BF16).astype(F32)
    wide = jnp.zeros((TOKENS, 128), F32)
    for k in range(TOP):
        wide = jnp.where(lane // FF == k, prob[:, k : k + 1], wide)
    scaled = jnp.where(lane < 64, wide * activated, 0.0).astype(BF16)
    erow = iota((128, 1024), 0)
    ecol = iota((128, 1024), 1)
    spread_to = ((erow % FF == ecol % FF) & (erow // FF == ecol // 128)).astype(BF16)
    tiled = dot(scaled, spread_to)
    routes = routes_ref[...].T
    spread = []
    for i in range(3):
        s = jnp.zeros((TOKENS, 128), F32)
        for k in range(TOP):
            s = jnp.where(lane // FF + 16 * i == routes[:, k : k + 1], tiled[:, 128 * k : 128 * k + 128], s)
        spread.append(s)
    spread = jnp.concatenate(spread, axis=1)[:, :320].astype(BF16)
    copies[0].wait()
    part_ref[...] = dot(spread, down_ref[...])
    keep_ref[...] = part_ref[pl.ds(pl.multiple_of(core * 64, 64), 64), :]
    send_ref[...] = part_ref[pl.ds(pl.multiple_of((1 - core) * 64, 64), 64), :]


def pair_body(keep_ref, got_ref, out_ref):
    v = (keep_ref[...] + got_ref[...]).astype(BF16)
    for i in range(8):
        out_ref[i] = v


def group_body(in_ref, out_ref):
    v = sum(in_ref[i].astype(F32) for i in range(8)).astype(BF16)
    for i in range(4):
        out_ref[i] = v


def finish_body(in_ref, res_ref, out_ref):
    core = lax.axis_index("core")
    own = res_ref[pl.ds(pl.multiple_of(core * 64, 64), 64), :]
    out_ref[...] = (own + sum(in_ref[i].astype(F32) for i in range(4))).astype(BF16)


def assemble_body(own_ref, other_ref, out_ref):
    core = lax.axis_index("core")
    out_ref[pl.ds(pl.multiple_of(core * 64, 64), 64), :] = own_ref[...]
    out_ref[pl.ds(pl.multiple_of((1 - core) * 64, 64), 64), :] = other_ref[...]


def swap(v):
    return lax.ppermute(v, "core", [(0, 1), (1, 0)])


def exchange(v, axes):
    return lax.all_to_all(v, axes, 0, 0, tiled=True)


def on_device(
    tokens,
    attn_gain,
    qkv_weight,
    out_weight,
    moe_gain,
    router_weight,
    expert_gate,
    expert_up,
    expert_down,
    cache_keys,
    cache_values,
    lengths,
    routes,
):
    z = ("zh", "zl")
    units = EXPERTS * FF
    (packed,) = call(
        attend_body,
        [((8, 32, 256), BF16)],
        (
            lengths,
            tokens,
            attn_gain,
            qkv_weight,
            cache_keys.reshape(REQS * SLOTS, 128),
            cache_values.reshape(REQS * SLOTS, 128),
        ),
        smem=(0,),
        raw=range(1, 6),
        scratch=[
            pltpu.VMEM((TOKENS, D), BF16),
            pltpu.VMEM((D,), F32),
            pltpu.VMEM((D, 640), BF16),
            pltpu.VMEM((REQS * SLOTS, 128), BF16),
            pltpu.VMEM((REQS * SLOTS, 128), BF16),
            pltpu.SemaphoreType.DMA((4 + CHUNKS,)),
        ],
    )
    (packed,) = call(merge_y_body, [((8, 32, 256), BF16)], (exchange(packed, ("y", "core")),))
    (packed,) = call(merge_z_body, [((16, 32, 256), BF16)], (exchange(packed, z),))
    mine = exchange(packed, ("y", "tp"))
    other = swap(mine)

    residual, picked = call(
        project_body,
        [((TOKENS, FEAT), F32), ((4, TOKENS, 256), BF16)],
        (
            mine,
            other,
            tokens,
            out_weight,
            moe_gain.reshape(1, FEAT),
            router_weight.T,
            expert_gate.transpose(0, 2, 1).reshape(units, FEAT),
            expert_up.transpose(0, 2, 1).reshape(units, FEAT),
            routes.T,
        ),
        raw=(6, 7),
        scratch=[pltpu.VMEM((units, FEAT), BF16)] * 2 + [pltpu.SemaphoreType.DMA((2,))],
    )
    half = ((TOKENS // 2, FEAT), F32)
    keep, send = call(
        expert_body,
        [half, half],
        (exchange(picked, "tp"), routes.T, expert_down.reshape(units, FEAT)),
        raw=(2,),
        scratch=[pltpu.VMEM((TOKENS, FEAT), F32), pltpu.VMEM((units, FEAT), BF16), pltpu.SemaphoreType.DMA((1,))],
    )
    (part,) = call(pair_body, [((8, TOKENS // 2, FEAT), BF16)], (keep, swap(send)))
    (part,) = call(group_body, [((4, TOKENS // 2, FEAT), BF16)], (exchange(part, ("zl", "y")),))
    (own,) = call(finish_body, [((TOKENS // 2, FEAT), BF16)], (exchange(part, "zh"), residual))
    (out,) = call(assemble_body, [((TOKENS, FEAT), BF16)], (own, swap(own)), pinned=False)
    return out


def solution(mesh):
    seq = ("zh", "zl", "y", "core")
    grid = Mesh(mesh.devices.reshape(4, 2, 4, 2, 4), seq + ("tp",))
    in_specs = (
        P(),
        P(),
        P(None, "tp"),
        P(None, "tp"),
        P("tp"),
        P("tp", None),
        P(None, "tp", seq),
        P(None, "tp", seq),
        P(None, seq, "tp"),
        P(None, seq, "tp"),
        P(None, seq, "tp"),
        P(),
        P(),
    )
    out_specs = P(None, "tp")
    return jax.shard_map(on_device, mesh=grid, in_specs=in_specs, out_specs=out_specs, check_vma=False)
```

```python
import functools

import jax
import jax.numpy as jnp
import numpy as np
from jax import lax
from jax.experimental import pallas as pl
from jax.experimental.pallas import tpu as pltpu
from jax.sharding import Mesh, PartitionSpec as P

D = 1536
HEAD = 64
EXPERTS = 40
TOP = 8
SINK = 4
NEW = 4
GROUP = 3
REQS = 32
TOKENS = 128
WINDOW = 2044
SLOTS = 32
FEAT = 384
FF = 8
CHUNKS = 4
HALF = TOKENS // 2

EPSILON = 1e-06
ROPE_BASE = 10000.0
FLOOR_SCORE = -1e30

F32 = jnp.float32
BF16 = jnp.bfloat16
VMEM = pl.BlockSpec(memory_space=pltpu.VMEM)
SMEM = pl.BlockSpec(memory_space=pltpu.SMEM)


def iota(shape, dim):
    return lax.broadcasted_iota(jnp.int32, shape, dim)


def dot(a, b):
    return jnp.dot(a, b, preferred_element_type=F32)


def dot_t(a, b):
    return lax.dot_general(a, b, (((1,), (1,)), ((), ())), preferred_element_type=F32)


def call(body, outs, args, smem=(), raw=(), scratch=(), pinned=True):
    kinds = ["s" if i in smem else "r" if i in raw else "v" for i in range(len(args))]
    run = pl.pallas_call(
        body,
        out_shape=[(pltpu.VMEM if pinned else jax.ShapeDtypeStruct)(shape, dtype) for shape, dtype in outs],
        in_specs=[{"s": SMEM, "r": pl.BlockSpec(memory_space=pl.ANY), "v": VMEM}[k] for k in kinds],
        out_specs=[VMEM for _ in outs],
        scratch_shapes=list(scratch),
        cost_estimate=pl.CostEstimate(flops=10**7, bytes_accessed=10**6, transcendentals=0),
    )
    space = {"s": pltpu.MemorySpace.SMEM, "r": pl.ANY, "v": pltpu.MemorySpace.VMEM}
    return run(*[pltpu.with_memory_space_constraint(a, space[k]) for a, k in zip(args, kinds)])


def started(pairs, sems):
    copies = [pltpu.make_async_copy(src, dst, sems.at[i]) for i, (src, dst) in enumerate(pairs)]
    for c in copies:
        c.start()
    return copies


def cos_sin(angle):
    turns = jnp.floor(angle * (2.0 / np.pi) + 0.5)
    r = angle - turns * QUARTER[0]
    r = r - turns * QUARTER[1]
    r = r - turns * QUARTER[2]
    r = r - turns * QUARTER[3]
    r2 = r * r
    sin = r + r * r2 * (-1.0 / 6 + r2 * (1.0 / 120 + r2 * (-1.0 / 5040 + r2 * (1.0 / 362880))))
    cos = 1.0 - 0.5 * r2 + r2 * r2 * (1.0 / 24 + r2 * (-1.0 / 720 + r2 * (1.0 / 40320 - r2 * (1.0 / 3628800))))
    which = turns.astype(jnp.int32) & 3
    odd = (which & 1) == 1
    c = jnp.where(odd, sin, cos)
    s = jnp.where(odd, cos, sin)
    return jnp.where((which == 1) | (which == 2), -c, c), jnp.where(which >= 2, -s, s)


def quarter_pieces():
    pieces = []
    rest = np.pi / 2
    for _ in range(3):
        top = np.floor(rest * 2.0 ** (7 - np.floor(np.log2(rest)))) / 2.0 ** (7 - np.floor(np.log2(rest)))
        pieces.append(float(top))
        rest = rest - top
    return pieces + [float(np.float32(rest))]


QUARTER = quarter_pieces()


def attend_body(
    len_ref,
    tok_hbm,
    gain_hbm,
    w_hbm,
    k_hbm,
    v_hbm,
    out_ref,
    tok_ref,
    gain_ref,
    w_ref,
    k_ref,
    v_ref,
    sems,
):
    part = D // CHUNKS
    pairs = [(tok_hbm, tok_ref), (gain_hbm, gain_ref)]
    pairs += [(w_hbm.at[pl.ds(i * part, part)], w_ref.at[pl.ds(i * part, part)]) for i in range(CHUNKS)]
    pairs += [(k_hbm, k_ref), (v_hbm, v_ref)]
    copies = started(pairs, sems)
    seq = ((lax.axis_index("zh") * 2 + lax.axis_index("zl")) * 4 + lax.axis_index("y")) * 2 + lax.axis_index("core")
    half = HEAD // 2
    spot = iota((8, 128), 1) % half
    freq = jnp.zeros((8, 128), F32)
    for i in range(half):
        freq = jnp.where(spot == i, float(np.float32(ROPE_BASE ** (-i / half))), freq)
    freq = freq[:1]
    copies[0].wait()
    copies[1].wait()
    x = tok_ref[...].astype(F32)
    normed = x * lax.rsqrt(jnp.mean(x * x, axis=-1, keepdims=True) + EPSILON) * gain_ref[...].reshape(1, D)
    normed = normed.astype(BF16)
    proj = jnp.zeros((TOKENS, 640), F32)
    for i in range(CHUNKS):
        copies[2 + i].wait()
        proj = proj + dot(normed[:, i * part : (i + 1) * part], w_ref[i * part : (i + 1) * part, :])
    copies[2 + CHUNKS].wait()
    copies[3 + CHUNKS].wait()
    lane = iota((32, 128), 1)
    row = iota((32, 128), 0)
    low = lane < 64
    first = (lane % 64) < 32
    slot = seq * SLOTS + lane % SLOTS
    nrow = iota((32, 32), 0)
    ncol = iota((32, 32), 1)
    ok_new = (nrow // NEW == ncol // NEW) & (ncol <= nrow) & (seq == 0)
    for grp in range(4):
        rows = slice(grp * 32, grp * 32 + 32)
        lens = jnp.zeros((32, 128), jnp.int32)
        for r in range(8):
            lens = jnp.where(row // NEW == r, len_ref[grp * 8 + r], lens)
        cos, sin = cos_sin((lens + row % NEW).astype(F32) * freq)
        sin = jnp.where(first, -sin, sin)
        tiles = [proj[rows, 128 * i : 128 * i + 128] for i in range(5)]
        turned = [t * cos + jnp.where(first, pltpu.roll(t, 96, 1), pltpu.roll(t, 32, 1)) * sin for t in tiles]
        query = []
        for g in range(2):
            for q in range(GROUP):
                at = g * 5 + q
                t = turned[at // 2]
                if at % 2 != g:
                    t = pltpu.roll(t, 64, 1)
                query.append(jnp.where(low if g == 0 else ~low, t * 0.125, 0.0).astype(BF16))
        qg = jnp.concatenate(query, axis=0)
        key_new = jnp.where(low, pltpu.roll(turned[1], 64, 1), pltpu.roll(turned[4], 64, 1)).astype(BF16)
        value_new = jnp.where(low, tiles[2], tiles[4]).astype(BF16)

        back = lens - 1 - slot
        safe = jnp.maximum(back, 0)
        age = safe - ((safe * 32833) >> 26) * WINDOW
        ok = (back >= 0) & ((slot < SINK) | (age <= WINDOW - 1 - row % NEW))
        ok = jnp.concatenate([ok & (row // NEW == lane // SLOTS + 4 * i) for i in range(2)], axis=1)
        s = dot_t(qg, k_ref[grp * 256 : grp * 256 + 256, :]).reshape(6, 32, 256)
        sn = dot_t(qg, key_new).reshape(6, 32, 32)
        s = jnp.where(ok[None], s, FLOOR_SCORE)
        sn = jnp.where(ok_new[None], sn, FLOOR_SCORE)
        m = jnp.maximum(jnp.max(s, axis=-1, keepdims=True), jnp.max(sn, axis=-1, keepdims=True))
        p = jnp.where(ok[None], jnp.exp(s - m), 0.0)
        pn = jnp.where(ok_new[None], jnp.exp(sn - m), 0.0)
        mass = jnp.sum(p, axis=-1, keepdims=True) + jnp.sum(pn, axis=-1, keepdims=True)
        acc = dot(p.reshape(192, 256).astype(BF16), v_ref[grp * 256 : grp * 256 + 256, :]) + dot(
            pn.reshape(192, 32).astype(BF16), value_new
        )
        some = mass > 0.0
        mass = jnp.where(some, mass, 1.0)
        acc = acc.reshape(6, 32, 128) / mass
        lse = jnp.where(some, m + jnp.log(mass), FLOOR_SCORE)
        for g in range(2):
            a = [acc[g * 3 + q] for q in range(3)]
            a = [b if q % 2 == g else pltpu.roll(b, 64, 1) for q, b in enumerate(a)]
            e = [lse[g * 3 + q] for q in range(3)]
            stats = jnp.where(lane == 64, e[0], jnp.where(lane == 65, e[1], jnp.where(lane == 66, e[2], 0.0)))
            lo, hi = encode(jnp.where(low, a[0], a[1]), a[2], stats)
            for c in range(2):
                out_ref[grp * 2 + c, :, 256 * g : 256 * g + 128] = lo[16 * c : 16 * c + 16]
                out_ref[grp * 2 + c, :, 256 * g + 128 : 256 * g + 256] = hi[16 * c : 16 * c + 16]


def merge(parts):
    top = functools.reduce(jnp.maximum, [e for _, _, e in parts])
    weights = [jnp.exp(e - top) for _, _, e in parts]
    total = sum(weights)
    lo = hi = 0.0
    glow = iota(total.shape, 1) < 64
    for w, (a, b, _) in zip(weights, parts):
        w = w / total
        lo = lo + a * jnp.where(glow, w[:, 64:65], w[:, 65:66])
        hi = hi + b * w[:, 66:67]
    return lo, hi, top + jnp.log(total)


def encode(lo, hi, lse):
    lane = iota(lse.shape, 1)
    a = lse.astype(BF16).astype(F32)
    b = (lse - a).astype(BF16).astype(F32)
    c = lse - a - b
    tail = jnp.where(lane < 67, a, jnp.where(lane < 70, pltpu.roll(b, 3, 1), pltpu.roll(c, 6, 1)))
    tail = jnp.where(lane < 73, tail, 0.0)
    return lo.astype(BF16), jnp.where(lane < 64, hi, tail).astype(BF16)


def decode(block):
    lo = block[:, :128].astype(F32)
    hi = block[:, 128:].astype(F32)
    lse = hi + pltpu.roll(hi, 125, 1) + pltpu.roll(hi, 122, 1)
    lane = iota(lse.shape, 1)
    return lo, hi, jnp.where((lane >= 64) & (lane < 67), lse, 0.0)


def merge_y_body(in_ref, out_ref):
    for g in range(2):
        at = slice(256 * g, 256 * g + 256)
        lo, hi = encode(*merge([decode(in_ref[i, :, at]) for i in range(8)]))
        for i in range(8):
            out_ref[i, :, 256 * g : 256 * g + 128] = lo
            out_ref[i, :, 256 * g + 128 : 256 * g + 256] = hi


def merge_z_body(in_ref, out_ref):
    heads = []
    for g in range(2):
        at = slice(256 * g, 256 * g + 256)
        heads.append(merge([decode(in_ref[i, :, at]) for i in range(8)]))
    low = iota((16, 128), 1) < 64
    last = jnp.where(low, heads[0][1], pltpu.roll(heads[1][1], 64, 1))
    for j, v in enumerate((heads[0][0], heads[1][0], last)):
        v = v.astype(BF16)
        for i in range(16):
            out_ref[i, :, 128 * j : 128 * j + 128] = v


def split3(v):
    a = v.astype(BF16)
    r = v - a.astype(F32)
    b = r.astype(BF16)
    return a, b, (r - b.astype(F32)).astype(BF16)


def own_rows(v, core):
    v = v.reshape(4, 32, v.shape[-1])
    return jnp.where(core == 0, v[:, :16], v[:, 16:]).reshape(HALF, v.shape[-1])


def project_body(
    mine_ref,
    w_ref,
    tok_ref,
    router_ref,
    routes_ref,
    gain_hbm,
    gate0_hbm,
    up0_hbm,
    gate1_hbm,
    up1_hbm,
    res_ref,
    out_ref,
    gate0_ref,
    up0_ref,
    gate1_ref,
    up1_ref,
    gain_ref,
    sems,
):
    core = lax.axis_index("core")
    tp = lax.axis_index("tp")
    pairs = [(gate0_hbm, gate0_ref), (up0_hbm, up0_ref), (gate1_hbm, gate1_ref), (up1_hbm, up1_ref)]
    pairs.append((gain_hbm, gain_ref))
    copies = started(pairs, sems)
    acc = jnp.zeros((HALF, FEAT), F32)
    for x in range(4):
        a = jnp.concatenate([mine_ref[y * 4 + x] for y in range(4)], axis=0)
        spans = [(0, 128), (192, 320), (128, 192), (320, 384)]
        w = jnp.concatenate([w_ref[384 * x + i : 384 * x + j, :] for i, j in spans], axis=0)
        acc = acc + dot(a, w)
    own = own_rows(tok_ref[:, pl.ds(pl.multiple_of(tp * FEAT, 128), FEAT)].astype(F32), core)
    acc = acc + own
    res_ref[...] = acc
    copies[4].wait()
    gained = acc * gain_ref[...].reshape(1, FEAT)
    squares = jnp.sum(acc * acc, axis=-1, keepdims=True)
    router = router_ref[...]
    g0, g1, g2 = split3(gained)
    logits = dot_t(g0, router) + dot_t(g1, router) + dot_t(g2, router)
    routes = own_rows(routes_ref[...].T, core)
    expert = (iota((HALF, 640), 1) % 320) // FF
    elane = iota((HALF, EXPERTS), 1)
    lane = iota((HALF, 128), 1)
    frow = iota((640, 128), 0)
    fcol = iota((640, 128), 1)
    fold = ((frow % FF == fcol % 64) & (frow // 320 == fcol // 64)).astype(BF16)
    stats = jnp.where(lane == TOP, squares, 0.0)
    for k in range(TOP):
        chosen = jnp.sum(jnp.where(elane == routes[:, k : k + 1], logits, 0.0), axis=-1, keepdims=True)
        stats = jnp.where(lane == k, chosen, stats)
    for c in copies[:4]:
        c.wait()
    both = [
        jnp.concatenate([dot_t(g0, gate0_ref[...]), dot_t(g0, up0_ref[...])], axis=1),
        jnp.concatenate([dot_t(g0, gate1_ref[...]), dot_t(g0, up1_ref[...])], axis=1),
    ]
    chosen = [expert == routes[:, k : k + 1] for k in range(TOP)]
    picks = []
    for v in both:
        v = jnp.concatenate([jnp.where(m, v, 0.0).astype(BF16) for m in chosen], axis=0)
        v = dot(v, fold).reshape(TOP, HALF, 128)
        picks.append(sum(v[k] if k == 0 else pltpu.roll(v[k], FF * k, 1) for k in range(TOP)))
    a, b, c = (v.astype(F32) for v in split3(stats))
    tail = (a + pltpu.roll(b, 16, 1) + pltpu.roll(c, 32, 1)).astype(BF16)
    for i in range(4):
        out_ref[i, :, :128] = picks[0].astype(BF16)
        out_ref[i, :, 128:256] = picks[1].astype(BF16)
        out_ref[i, :, 256:] = tail


def expert_body(in_ref, routes_ref, down0_hbm, down1_hbm, out_ref, down0_ref, down1_ref, sems):
    core = lax.axis_index("core")
    copies = started([(down0_hbm, down0_ref), (down1_hbm, down1_ref)], sems)
    lane = iota((HALF, 128), 1)
    tail = sum(in_ref[i, :, 256:].astype(F32) for i in range(4))
    stats = tail + pltpu.roll(tail, 112, 1) + pltpu.roll(tail, 96, 1)
    scale = lax.rsqrt(stats[:, TOP : TOP + 1] / D + EPSILON)
    logits = jnp.where(lane < TOP, stats * scale, FLOOR_SCORE)
    weights = jnp.exp(logits - jnp.max(logits, axis=-1, keepdims=True))
    prob = weights / jnp.sum(weights, axis=-1, keepdims=True)
    wide = jnp.zeros((HALF, 128), F32)
    for k in range(TOP):
        wide = jnp.where(lane // FF == k, prob[:, k : k + 1], wide)
    erow = iota((128, 1024), 0)
    ecol = iota((128, 1024), 1)
    spread_to = ((erow % FF == ecol % FF) & (erow // FF == ecol // 128)).astype(BF16)
    tiled = []
    for j in range(2):
        gate = scale * sum(in_ref[i, :, 128 * j : 128 * j + 128].astype(F32) for i in range(4))
        up = pltpu.roll(gate, 64, 1)
        activated = (gate / (1.0 + jnp.exp(-gate)) * up).astype(BF16).astype(F32)
        tiled.append(dot(jnp.where(lane < 64, wide * activated, 0.0).astype(BF16), spread_to))
    routes = own_rows(routes_ref[...].T, core)
    part = jnp.zeros((HALF, FEAT), F32)
    for t, down_ref, copy in zip(tiled, (down0_ref, down1_ref), copies):
        spread = []
        for i in range(3):
            s = jnp.zeros((HALF, 128), F32)
            for k in range(TOP):
                s = jnp.where(lane // FF + 16 * i == routes[:, k : k + 1], t[:, 128 * k : 128 * k + 128], s)
            spread.append(s)
        spread = jnp.concatenate(spread, axis=1)[:, :320].astype(BF16)
        copy.wait()
        part = part + dot(spread, down_ref[...])
    for i in range(8):
        out_ref[i] = part.astype(BF16)


def group_body(in_ref, out_ref):
    v = sum(in_ref[i].astype(F32) for i in range(8)).astype(BF16)
    for i in range(4):
        out_ref[i] = v


def finish_body(in_ref, res_ref, out_ref):
    out_ref[...] = (res_ref[...] + sum(in_ref[i].astype(F32) for i in range(4))).astype(BF16)


def assemble_body(own_ref, other_ref, out_ref):
    core = lax.axis_index("core")
    for y in range(4):
        rows = slice(16 * y, 16 * y + 16)
        out_ref[pl.ds(pl.multiple_of(y * 32 + core * 16, 16), 16), :] = own_ref[rows]
        out_ref[pl.ds(pl.multiple_of(y * 32 + (1 - core) * 16, 16), 16), :] = other_ref[rows]


def swap(v):
    return lax.ppermute(v, "core", [(0, 1), (1, 0)])


def exchange(v, axes):
    return lax.all_to_all(v, axes, 0, 0, tiled=True)


def on_device(
    tokens,
    attn_gain,
    qkv_weight,
    out_weight,
    moe_gain,
    router_weight,
    expert_gate,
    expert_up,
    expert_down,
    cache_keys,
    cache_values,
    lengths,
    routes,
):
    z = ("zh", "zl")
    units = EXPERTS * FF
    gate = expert_gate.transpose(0, 2, 1).reshape(units, FEAT)
    up = expert_up.transpose(0, 2, 1).reshape(units, FEAT)
    down = expert_down.reshape(units, FEAT)
    gate_there, up_there, down_there = swap(gate), swap(up), swap(down)
    (packed,) = call(
        attend_body,
        [((8, 16, 512), BF16)],
        (
            lengths,
            tokens,
            attn_gain,
            qkv_weight,
            cache_keys.reshape(REQS * SLOTS, 128),
            cache_values.reshape(REQS * SLOTS, 128),
        ),
        smem=(0,),
        raw=range(1, 6),
        scratch=[
            pltpu.VMEM((TOKENS, D), BF16),
            pltpu.VMEM((D,), F32),
            pltpu.VMEM((D, 640), BF16),
            pltpu.VMEM((REQS * SLOTS, 128), BF16),
            pltpu.VMEM((REQS * SLOTS, 128), BF16),
            pltpu.SemaphoreType.DMA((4 + CHUNKS,)),
        ],
    )
    packed, gate_there, up_there, down_there = lax.optimization_barrier((packed, gate_there, up_there, down_there))
    (packed,) = call(merge_y_body, [((8, 16, 512), BF16)], (exchange(packed, ("y", "core")),))
    (packed,) = call(merge_z_body, [((16, 16, 384), BF16)], (exchange(packed, z),))
    residual, picked = call(
        project_body,
        [((HALF, FEAT), F32), ((4, HALF, 384), BF16)],
        (
            exchange(packed, ("y", "tp")),
            out_weight,
            tokens,
            router_weight.T,
            routes.T,
            moe_gain,
            gate,
            up,
            gate_there,
            up_there,
        ),
        raw=(5, 6, 7, 8, 9),
        scratch=[pltpu.VMEM((units, FEAT), BF16)] * 4 + [pltpu.VMEM((FEAT,), F32), pltpu.SemaphoreType.DMA((5,))],
    )
    (part,) = call(
        expert_body,
        [((8, HALF, FEAT), BF16)],
        (exchange(picked, "tp"), routes.T, down, down_there),
        raw=(2, 3),
        scratch=[pltpu.VMEM((units, FEAT), BF16)] * 2 + [pltpu.SemaphoreType.DMA((2,))],
    )
    (part,) = call(group_body, [((4, HALF, FEAT), BF16)], (exchange(part, ("zl", "y")),))
    (own,) = call(finish_body, [((HALF, FEAT), BF16)], (exchange(part, "zh"), residual))
    (out,) = call(assemble_body, [((TOKENS, FEAT), BF16)], (own, swap(own)), pinned=False)
    return out


def solution(mesh):
    seq = ("zh", "zl", "y", "core")
    grid = Mesh(mesh.devices.reshape(4, 2, 4, 2, 4), seq + ("tp",))
    in_specs = (
        P(),
        P(),
        P(None, "tp"),
        P(None, "tp"),
        P("tp"),
        P("tp", None),
        P(None, "tp", seq),
        P(None, "tp", seq),
        P(None, seq, "tp"),
        P(None, seq, "tp"),
        P(None, seq, "tp"),
        P(),
        P(),
    )
    out_specs = P(None, "tp")
    return jax.shard_map(on_device, mesh=grid, in_specs=in_specs, out_specs=out_specs, check_vma=False)
```

```python
import functools

import jax
import jax.numpy as jnp
import numpy as np
from jax import lax
from jax.experimental import pallas as pl
from jax.experimental.pallas import tpu as pltpu
from jax.sharding import Mesh, PartitionSpec as P

D = 1536
HEAD = 64
EXPERTS = 40
TOP = 8
SINK = 4
NEW = 4
GROUP = 3
REQS = 32
TOKENS = 128
WINDOW = 2044
SLOTS = 32
FEAT = 384
FF = 8
CHUNKS = 4
HALF = TOKENS // 2

EPSILON = 1e-06
ROPE_BASE = 10000.0
FLOOR_SCORE = -1e30

F32 = jnp.float32
BF16 = jnp.bfloat16
VMEM = pl.BlockSpec(memory_space=pltpu.VMEM)
SMEM = pl.BlockSpec(memory_space=pltpu.SMEM)


def iota(shape, dim):
    return lax.broadcasted_iota(jnp.int32, shape, dim)


def dot(a, b):
    return jnp.dot(a, b, preferred_element_type=F32)


def dot_t(a, b):
    return lax.dot_general(a, b, (((1,), (1,)), ((), ())), preferred_element_type=F32)


def call(body, outs, args, smem=(), raw=(), scratch=(), pinned=True):
    kinds = ["s" if i in smem else "r" if i in raw else "v" for i in range(len(args))]
    run = pl.pallas_call(
        body,
        out_shape=[(pltpu.VMEM if pinned else jax.ShapeDtypeStruct)(shape, dtype) for shape, dtype in outs],
        in_specs=[{"s": SMEM, "r": pl.BlockSpec(memory_space=pl.ANY), "v": VMEM}[k] for k in kinds],
        out_specs=[VMEM for _ in outs],
        scratch_shapes=list(scratch),
        cost_estimate=pl.CostEstimate(flops=10**7, bytes_accessed=10**6, transcendentals=0),
    )
    space = {"s": pltpu.MemorySpace.SMEM, "r": pl.ANY, "v": pltpu.MemorySpace.VMEM}
    return run(*[pltpu.with_memory_space_constraint(a, space[k]) for a, k in zip(args, kinds)])


def started(pairs, sems):
    copies = [pltpu.make_async_copy(src, dst, sems.at[i]) for i, (src, dst) in enumerate(pairs)]
    for c in copies:
        c.start()
    return copies


def cos_sin(angle):
    turns = jnp.floor(angle * (2.0 / np.pi) + 0.5)
    r = angle - turns * QUARTER[0]
    r = r - turns * QUARTER[1]
    r = r - turns * QUARTER[2]
    r = r - turns * QUARTER[3]
    r2 = r * r
    sin = r + r * r2 * (-1.0 / 6 + r2 * (1.0 / 120 + r2 * (-1.0 / 5040 + r2 * (1.0 / 362880))))
    cos = 1.0 - 0.5 * r2 + r2 * r2 * (1.0 / 24 + r2 * (-1.0 / 720 + r2 * (1.0 / 40320 - r2 * (1.0 / 3628800))))
    which = turns.astype(jnp.int32) & 3
    odd = (which & 1) == 1
    c = jnp.where(odd, sin, cos)
    s = jnp.where(odd, cos, sin)
    return jnp.where((which == 1) | (which == 2), -c, c), jnp.where(which >= 2, -s, s)


def quarter_pieces():
    pieces = []
    rest = np.pi / 2
    for _ in range(3):
        top = np.floor(rest * 2.0 ** (7 - np.floor(np.log2(rest)))) / 2.0 ** (7 - np.floor(np.log2(rest)))
        pieces.append(float(top))
        rest = rest - top
    return pieces + [float(np.float32(rest))]


QUARTER = quarter_pieces()


def attend_body(
    len_ref,
    tok_hbm,
    gain_hbm,
    w_hbm,
    k_hbm,
    v_hbm,
    out_ref,
    tok_ref,
    gain_ref,
    w_ref,
    k_ref,
    v_ref,
    sems,
):
    part = D // CHUNKS
    pairs = [(tok_hbm, tok_ref), (gain_hbm, gain_ref)]
    pairs += [(w_hbm.at[pl.ds(i * part, part)], w_ref.at[pl.ds(i * part, part)]) for i in range(CHUNKS)]
    pairs += [(k_hbm, k_ref), (v_hbm, v_ref)]
    copies = started(pairs, sems)
    seq = ((lax.axis_index("zh") * 2 + lax.axis_index("zl")) * 4 + lax.axis_index("y")) * 2 + lax.axis_index("core")
    half = HEAD // 2
    spot = iota((8, 128), 1) % half
    freq = jnp.zeros((8, 128), F32)
    for i in range(half):
        freq = jnp.where(spot == i, float(np.float32(ROPE_BASE ** (-i / half))), freq)
    freq = freq[:1]
    copies[0].wait()
    copies[1].wait()
    x = tok_ref[...].astype(F32)
    normed = x * lax.rsqrt(jnp.mean(x * x, axis=-1, keepdims=True) + EPSILON) * gain_ref[...].reshape(1, D)
    normed = normed.astype(BF16)
    proj = jnp.zeros((TOKENS, 640), F32)
    for i in range(CHUNKS):
        copies[2 + i].wait()
        proj = proj + dot(normed[:, i * part : (i + 1) * part], w_ref[i * part : (i + 1) * part, :])
    copies[2 + CHUNKS].wait()
    copies[3 + CHUNKS].wait()
    lane = iota((32, 128), 1)
    row = iota((32, 128), 0)
    low = lane < 64
    first = (lane % 64) < 32
    slot = seq * SLOTS + lane % SLOTS
    nrow = iota((32, 32), 0)
    ncol = iota((32, 32), 1)
    ok_new = (nrow // NEW == ncol // NEW) & (ncol <= nrow) & (seq == 0)
    for grp in range(4):
        rows = slice(grp * 32, grp * 32 + 32)
        lens = jnp.zeros((32, 128), jnp.int32)
        for r in range(8):
            lens = jnp.where(row // NEW == r, len_ref[grp * 8 + r], lens)
        cos, sin = cos_sin((lens + row % NEW).astype(F32) * freq)
        sin = jnp.where(first, -sin, sin)
        tiles = [proj[rows, 128 * i : 128 * i + 128] for i in range(5)]
        turned = [t * cos + jnp.where(first, pltpu.roll(t, 96, 1), pltpu.roll(t, 32, 1)) * sin for t in tiles]
        query = []
        for g in range(2):
            for q in range(GROUP):
                at = g * 5 + q
                t = turned[at // 2]
                if at % 2 != g:
                    t = pltpu.roll(t, 64, 1)
                query.append(jnp.where(low if g == 0 else ~low, t * 0.125, 0.0).astype(BF16))
        qg = jnp.concatenate(query, axis=0)
        key_new = jnp.where(low, pltpu.roll(turned[1], 64, 1), pltpu.roll(turned[4], 64, 1)).astype(BF16)
        value_new = jnp.where(low, tiles[2], tiles[4]).astype(BF16)

        back = lens - 1 - slot
        safe = jnp.maximum(back, 0)
        age = safe - ((safe * 32833) >> 26) * WINDOW
        ok = (back >= 0) & ((slot < SINK) | (age <= WINDOW - 1 - row % NEW))
        ok = jnp.concatenate([ok & (row // NEW == lane // SLOTS + 4 * i) for i in range(2)], axis=1)
        s = dot_t(qg, k_ref[grp * 256 : grp * 256 + 256, :]).reshape(6, 32, 256)
        sn = dot_t(qg, key_new).reshape(6, 32, 32)
        s = jnp.where(ok[None], s, FLOOR_SCORE)
        sn = jnp.where(ok_new[None], sn, FLOOR_SCORE)
        m = jnp.maximum(jnp.max(s, axis=-1, keepdims=True), jnp.max(sn, axis=-1, keepdims=True))
        p = jnp.where(ok[None], jnp.exp(s - m), 0.0)
        pn = jnp.where(ok_new[None], jnp.exp(sn - m), 0.0)
        mass = jnp.sum(p, axis=-1, keepdims=True) + jnp.sum(pn, axis=-1, keepdims=True)
        acc = dot(p.reshape(192, 256).astype(BF16), v_ref[grp * 256 : grp * 256 + 256, :]) + dot(
            pn.reshape(192, 32).astype(BF16), value_new
        )
        some = mass > 0.0
        mass = jnp.where(some, mass, 1.0)
        acc = acc.reshape(6, 32, 128) / mass
        lse = jnp.where(some, m + jnp.log(mass), FLOOR_SCORE)
        for g in range(2):
            a = [acc[g * 3 + q] for q in range(3)]
            a = [b if q % 2 == g else pltpu.roll(b, 64, 1) for q, b in enumerate(a)]
            e = [lse[g * 3 + q] for q in range(3)]
            stats = jnp.where(lane == 64, e[0], jnp.where(lane == 65, e[1], jnp.where(lane == 66, e[2], 0.0)))
            lo, hi = encode(jnp.where(low, a[0], a[1]), a[2], stats)
            for c in range(2):
                out_ref[grp * 2 + c, :, 256 * g : 256 * g + 128] = lo[16 * c : 16 * c + 16]
                out_ref[grp * 2 + c, :, 256 * g + 128 : 256 * g + 256] = hi[16 * c : 16 * c + 16]


def merge(parts):
    top = functools.reduce(jnp.maximum, [e for _, _, e in parts])
    weights = [jnp.exp(e - top) for _, _, e in parts]
    total = sum(weights)
    lo = hi = 0.0
    glow = iota(total.shape, 1) < 64
    for w, (a, b, _) in zip(weights, parts):
        w = w / total
        lo = lo + a * jnp.where(glow, w[:, 64:65], w[:, 65:66])
        hi = hi + b * w[:, 66:67]
    return lo, hi, top + jnp.log(total)


def encode(lo, hi, lse):
    lane = iota(lse.shape, 1)
    a = lse.astype(BF16).astype(F32)
    b = (lse - a).astype(BF16).astype(F32)
    c = lse - a - b
    tail = jnp.where(lane < 67, a, jnp.where(lane < 70, pltpu.roll(b, 3, 1), pltpu.roll(c, 6, 1)))
    tail = jnp.where(lane < 73, tail, 0.0)
    return lo.astype(BF16), jnp.where(lane < 64, hi, tail).astype(BF16)


def decode(block):
    lo = block[:, :128].astype(F32)
    hi = block[:, 128:].astype(F32)
    lse = hi + pltpu.roll(hi, 125, 1) + pltpu.roll(hi, 122, 1)
    lane = iota(lse.shape, 1)
    return lo, hi, jnp.where((lane >= 64) & (lane < 67), lse, 0.0)


def merge_y_body(in_ref, out_ref):
    for g in range(2):
        at = slice(256 * g, 256 * g + 256)
        lo, hi = encode(*merge([decode(in_ref[i, :, at]) for i in range(8)]))
        for i in range(8):
            out_ref[i, :, 256 * g : 256 * g + 128] = lo
            out_ref[i, :, 256 * g + 128 : 256 * g + 256] = hi


def merge_z_body(in_ref, out_ref):
    heads = []
    for g in range(2):
        at = slice(256 * g, 256 * g + 256)
        heads.append(merge([decode(in_ref[i, :, at]) for i in range(8)]))
    low = iota((16, 128), 1) < 64
    last = jnp.where(low, heads[0][1], pltpu.roll(heads[1][1], 64, 1))
    for j, v in enumerate((heads[0][0], heads[1][0], last)):
        v = v.astype(BF16)
        for i in range(16):
            out_ref[i, :, 128 * j : 128 * j + 128] = v


def split3(v):
    a = v.astype(BF16)
    r = v - a.astype(F32)
    b = r.astype(BF16)
    return a, b, (r - b.astype(F32)).astype(BF16)


def own_rows(v, core):
    v = v.reshape(4, 32, v.shape[-1])
    return jnp.where(core == 0, v[:, :16], v[:, 16:]).reshape(HALF, v.shape[-1])


def project_body(
    mine_ref,
    w_ref,
    tok_ref,
    router_ref,
    routes_ref,
    gate1_ref,
    up1_ref,
    gain_hbm,
    gate0_hbm,
    up0_hbm,
    res_ref,
    out_ref,
    gate0_ref,
    up0_ref,
    gain_ref,
    sems,
):
    core = lax.axis_index("core")
    tp = lax.axis_index("tp")
    pairs = [(gate0_hbm, gate0_ref), (up0_hbm, up0_ref), (gain_hbm, gain_ref)]
    copies = started(pairs, sems)
    acc = jnp.zeros((HALF, FEAT), F32)
    for x in range(4):
        a = jnp.concatenate([mine_ref[y * 4 + x] for y in range(4)], axis=0)
        spans = [(0, 128), (192, 320), (128, 192), (320, 384)]
        w = jnp.concatenate([w_ref[384 * x + i : 384 * x + j, :] for i, j in spans], axis=0)
        acc = acc + dot(a, w)
    own = own_rows(tok_ref[:, pl.ds(pl.multiple_of(tp * FEAT, 128), FEAT)].astype(F32), core)
    acc = acc + own
    res_ref[...] = acc
    copies[2].wait()
    gained = acc * gain_ref[...].reshape(1, FEAT)
    squares = jnp.sum(acc * acc, axis=-1, keepdims=True)
    router = router_ref[...]
    g0, g1, g2 = split3(gained)
    logits = dot_t(g0, router) + dot_t(g1, router) + dot_t(g2, router)
    routes = own_rows(routes_ref[...].T, core)
    expert = (iota((HALF, 640), 1) % 320) // FF
    elane = iota((HALF, EXPERTS), 1)
    lane = iota((HALF, 128), 1)
    frow = iota((640, 128), 0)
    fcol = iota((640, 128), 1)
    fold = ((frow % FF == fcol % 64) & (frow // 320 == fcol // 64)).astype(BF16)
    stats = jnp.where(lane == TOP, squares, 0.0)
    for k in range(TOP):
        chosen = jnp.sum(jnp.where(elane == routes[:, k : k + 1], logits, 0.0), axis=-1, keepdims=True)
        stats = jnp.where(lane == k, chosen, stats)
    for c in copies[:2]:
        c.wait()
    both = [
        jnp.concatenate([dot_t(g0, gate0_ref[...]), dot_t(g0, up0_ref[...])], axis=1),
        jnp.concatenate([dot_t(g0, gate1_ref[...]), dot_t(g0, up1_ref[...])], axis=1),
    ]
    chosen = [expert == routes[:, k : k + 1] for k in range(TOP)]
    picks = []
    for v in both:
        v = jnp.concatenate([jnp.where(m, v, 0.0).astype(BF16) for m in chosen], axis=0)
        v = dot(v, fold).reshape(TOP, HALF, 128)
        picks.append(sum(v[k] if k == 0 else pltpu.roll(v[k], FF * k, 1) for k in range(TOP)))
    a, b, c = (v.astype(F32) for v in split3(stats))
    tail = (a + pltpu.roll(b, 16, 1) + pltpu.roll(c, 32, 1)).astype(BF16)
    for i in range(4):
        out_ref[i, :, :128] = picks[0].astype(BF16)
        out_ref[i, :, 128:256] = picks[1].astype(BF16)
        out_ref[i, :, 256:] = tail


def expert_body(in_ref, routes_ref, down1_ref, down0_hbm, out_ref, down0_ref, sems):
    core = lax.axis_index("core")
    copies = started([(down0_hbm, down0_ref)], sems)
    lane = iota((HALF, 128), 1)
    tail = sum(in_ref[i, :, 256:].astype(F32) for i in range(4))
    stats = tail + pltpu.roll(tail, 112, 1) + pltpu.roll(tail, 96, 1)
    scale = lax.rsqrt(stats[:, TOP : TOP + 1] / D + EPSILON)
    logits = jnp.where(lane < TOP, stats * scale, FLOOR_SCORE)
    weights = jnp.exp(logits - jnp.max(logits, axis=-1, keepdims=True))
    prob = weights / jnp.sum(weights, axis=-1, keepdims=True)
    wide = jnp.zeros((HALF, 128), F32)
    for k in range(TOP):
        wide = jnp.where(lane // FF == k, prob[:, k : k + 1], wide)
    erow = iota((128, 1024), 0)
    ecol = iota((128, 1024), 1)
    spread_to = ((erow % FF == ecol % FF) & (erow // FF == ecol // 128)).astype(BF16)
    tiled = []
    for j in range(2):
        gate = scale * sum(in_ref[i, :, 128 * j : 128 * j + 128].astype(F32) for i in range(4))
        up = pltpu.roll(gate, 64, 1)
        activated = (gate / (1.0 + jnp.exp(-gate)) * up).astype(BF16).astype(F32)
        tiled.append(dot(jnp.where(lane < 64, wide * activated, 0.0).astype(BF16), spread_to))
    routes = own_rows(routes_ref[...].T, core)
    part = jnp.zeros((HALF, FEAT), F32)
    for t, down_ref in zip(tiled[::-1], (down1_ref, down0_ref)):
        spread = []
        for i in range(3):
            s = jnp.zeros((HALF, 128), F32)
            for k in range(TOP):
                s = jnp.where(lane // FF + 16 * i == routes[:, k : k + 1], t[:, 128 * k : 128 * k + 128], s)
            spread.append(s)
        spread = jnp.concatenate(spread, axis=1)[:, :320].astype(BF16)
        if down_ref is down0_ref:
            copies[0].wait()
        part = part + dot(spread, down_ref[...])
    for i in range(8):
        out_ref[i] = part.astype(BF16)


def group_body(in_ref, out_ref):
    v = sum(in_ref[i].astype(F32) for i in range(8)).astype(BF16)
    for i in range(4):
        out_ref[i] = v


def finish_body(in_ref, res_ref, out_ref):
    out_ref[...] = (res_ref[...] + sum(in_ref[i].astype(F32) for i in range(4))).astype(BF16)


def assemble_body(own_ref, other_ref, out_ref):
    core = lax.axis_index("core")
    for y in range(4):
        rows = slice(16 * y, 16 * y + 16)
        out_ref[pl.ds(pl.multiple_of(y * 32 + core * 16, 16), 16), :] = own_ref[rows]
        out_ref[pl.ds(pl.multiple_of(y * 32 + (1 - core) * 16, 16), 16), :] = other_ref[rows]


def swap(v):
    return lax.ppermute(v, "core", [(0, 1), (1, 0)])


def exchange(v, axes):
    return lax.all_to_all(v, axes, 0, 0, tiled=True)


def on_device(
    tokens,
    attn_gain,
    qkv_weight,
    out_weight,
    moe_gain,
    router_weight,
    expert_gate,
    expert_up,
    expert_down,
    cache_keys,
    cache_values,
    lengths,
    routes,
):
    z = ("zh", "zl")
    units = EXPERTS * FF
    gate = expert_gate.transpose(0, 2, 1).reshape(units, FEAT)
    up = expert_up.transpose(0, 2, 1).reshape(units, FEAT)
    down = expert_down.reshape(units, FEAT)
    gate_there, up_there, down_there = swap(gate), swap(up), swap(down)
    (packed,) = call(
        attend_body,
        [((8, 16, 512), BF16)],
        (
            lengths,
            tokens,
            attn_gain,
            qkv_weight,
            cache_keys.reshape(REQS * SLOTS, 128),
            cache_values.reshape(REQS * SLOTS, 128),
        ),
        smem=(0,),
        raw=range(1, 6),
        scratch=[
            pltpu.VMEM((TOKENS, D), BF16),
            pltpu.VMEM((D,), F32),
            pltpu.VMEM((D, 640), BF16),
            pltpu.VMEM((REQS * SLOTS, 128), BF16),
            pltpu.VMEM((REQS * SLOTS, 128), BF16),
            pltpu.SemaphoreType.DMA((4 + CHUNKS,)),
        ],
    )
    packed, gate_there, up_there, down_there = lax.optimization_barrier((packed, gate_there, up_there, down_there))
    (packed,) = call(merge_y_body, [((8, 16, 512), BF16)], (exchange(packed, ("y", "core")),))
    (packed,) = call(merge_z_body, [((16, 16, 384), BF16)], (exchange(packed, z),))
    residual, picked = call(
        project_body,
        [((HALF, FEAT), F32), ((4, HALF, 384), BF16)],
        (
            exchange(packed, ("y", "tp")),
            out_weight,
            tokens,
            router_weight.T,
            routes.T,
            gate_there,
            up_there,
            moe_gain,
            gate,
            up,
        ),
        raw=(7, 8, 9),
        scratch=[pltpu.VMEM((units, FEAT), BF16)] * 2 + [pltpu.VMEM((FEAT,), F32), pltpu.SemaphoreType.DMA((3,))],
    )
    (part,) = call(
        expert_body,
        [((8, HALF, FEAT), BF16)],
        (exchange(picked, "tp"), routes.T, down_there, down),
        raw=(3,),
        scratch=[pltpu.VMEM((units, FEAT), BF16), pltpu.SemaphoreType.DMA((1,))],
    )
    (part,) = call(group_body, [((4, HALF, FEAT), BF16)], (exchange(part, ("zl", "y")),))
    (own,) = call(finish_body, [((HALF, FEAT), BF16)], (exchange(part, "zh"), residual))
    (out,) = call(assemble_body, [((TOKENS, FEAT), BF16)], (own, swap(own)), pinned=False)
    return out


def solution(mesh):
    seq = ("zh", "zl", "y", "core")
    grid = Mesh(mesh.devices.reshape(4, 2, 4, 2, 4), seq + ("tp",))
    in_specs = (
        P(),
        P(),
        P(None, "tp"),
        P(None, "tp"),
        P("tp"),
        P("tp", None),
        P(None, "tp", seq),
        P(None, "tp", seq),
        P(None, seq, "tp"),
        P(None, seq, "tp"),
        P(None, seq, "tp"),
        P(),
        P(),
    )
    out_specs = P(None, "tp")
    return jax.shard_map(on_device, mesh=grid, in_specs=in_specs, out_specs=out_specs, check_vma=False)
```

```python
import functools

import jax
import jax.numpy as jnp
import numpy as np
from jax import lax
from jax.experimental import pallas as pl
from jax.experimental.pallas import tpu as pltpu
from jax.sharding import Mesh, PartitionSpec as P

D = 1536
HEAD = 64
EXPERTS = 40
TOP = 8
SINK = 4
NEW = 4
GROUP = 3
REQS = 32
TOKENS = 128
WINDOW = 2044
SLOTS = 32
FEAT = 384
FF = 8
CHUNKS = 4
HALF = TOKENS // 2

EPSILON = 1e-06
ROPE_BASE = 10000.0
FLOOR_SCORE = -1e30

F32 = jnp.float32
BF16 = jnp.bfloat16
VMEM = pl.BlockSpec(memory_space=pltpu.VMEM)
SMEM = pl.BlockSpec(memory_space=pltpu.SMEM)


def iota(shape, dim):
    return lax.broadcasted_iota(jnp.int32, shape, dim)


def dot(a, b):
    return jnp.dot(a, b, preferred_element_type=F32)


def dot_t(a, b):
    return lax.dot_general(a, b, (((1,), (1,)), ((), ())), preferred_element_type=F32)


def call(body, outs, args, smem=(), raw=(), scratch=(), pinned=True):
    kinds = ["s" if i in smem else "r" if i in raw else "v" for i in range(len(args))]
    run = pl.pallas_call(
        body,
        out_shape=[(pltpu.VMEM if pinned else jax.ShapeDtypeStruct)(shape, dtype) for shape, dtype in outs],
        in_specs=[{"s": SMEM, "r": pl.BlockSpec(memory_space=pl.ANY), "v": VMEM}[k] for k in kinds],
        out_specs=[VMEM for _ in outs],
        scratch_shapes=list(scratch),
        cost_estimate=pl.CostEstimate(flops=10**7, bytes_accessed=10**6, transcendentals=0),
    )
    space = {"s": pltpu.MemorySpace.SMEM, "r": pl.ANY, "v": pltpu.MemorySpace.VMEM}
    return run(*[pltpu.with_memory_space_constraint(a, space[k]) for a, k in zip(args, kinds)])


def started(pairs, sems):
    copies = [pltpu.make_async_copy(src, dst, sems.at[i]) for i, (src, dst) in enumerate(pairs)]
    for c in copies:
        c.start()
    return copies


def cos_sin(angle):
    turns = jnp.floor(angle * (2.0 / np.pi) + 0.5)
    r = angle - turns * QUARTER[0]
    r = r - turns * QUARTER[1]
    r = r - turns * QUARTER[2]
    r = r - turns * QUARTER[3]
    r2 = r * r
    sin = r + r * r2 * (-1.0 / 6 + r2 * (1.0 / 120 + r2 * (-1.0 / 5040 + r2 * (1.0 / 362880))))
    cos = 1.0 - 0.5 * r2 + r2 * r2 * (1.0 / 24 + r2 * (-1.0 / 720 + r2 * (1.0 / 40320 - r2 * (1.0 / 3628800))))
    which = turns.astype(jnp.int32) & 3
    odd = (which & 1) == 1
    c = jnp.where(odd, sin, cos)
    s = jnp.where(odd, cos, sin)
    return jnp.where((which == 1) | (which == 2), -c, c), jnp.where(which >= 2, -s, s)


def quarter_pieces():
    pieces = []
    rest = np.pi / 2
    for _ in range(3):
        top = np.floor(rest * 2.0 ** (7 - np.floor(np.log2(rest)))) / 2.0 ** (7 - np.floor(np.log2(rest)))
        pieces.append(float(top))
        rest = rest - top
    return pieces + [float(np.float32(rest))]


QUARTER = quarter_pieces()


def attend_body(
    len_ref,
    tok_hbm,
    gain_hbm,
    w_hbm,
    k_hbm,
    v_hbm,
    out_ref,
    tok_ref,
    gain_ref,
    w_ref,
    k_ref,
    v_ref,
    sems,
):
    part = D // CHUNKS
    pairs = [(tok_hbm, tok_ref), (gain_hbm, gain_ref)]
    pairs += [(w_hbm.at[pl.ds(i * part, part)], w_ref.at[pl.ds(i * part, part)]) for i in range(CHUNKS)]
    pairs += [(k_hbm, k_ref), (v_hbm, v_ref)]
    copies = started(pairs, sems)
    seq = ((lax.axis_index("zh") * 2 + lax.axis_index("zl")) * 4 + lax.axis_index("y")) * 2 + lax.axis_index("core")
    half = HEAD // 2
    spot = iota((8, 128), 1) % half
    freq = jnp.zeros((8, 128), F32)
    for i in range(half):
        freq = jnp.where(spot == i, float(np.float32(ROPE_BASE ** (-i / half))), freq)
    freq = freq[:1]
    copies[0].wait()
    copies[1].wait()
    x = tok_ref[...].astype(F32)
    normed = x * lax.rsqrt(jnp.mean(x * x, axis=-1, keepdims=True) + EPSILON) * gain_ref[...].reshape(1, D)
    normed = normed.astype(BF16)
    proj = jnp.zeros((TOKENS, 640), F32)
    for i in range(CHUNKS):
        copies[2 + i].wait()
        proj = proj + dot(normed[:, i * part : (i + 1) * part], w_ref[i * part : (i + 1) * part, :])
    copies[2 + CHUNKS].wait()
    copies[3 + CHUNKS].wait()
    lane = iota((32, 128), 1)
    row = iota((32, 128), 0)
    low = lane < 64
    first = (lane % 64) < 32
    slot = seq * SLOTS + lane % SLOTS
    nrow = iota((32, 32), 0)
    ncol = iota((32, 32), 1)
    ok_new = (nrow // NEW == ncol // NEW) & (ncol <= nrow) & (seq == 0)
    for grp in range(4):
        rows = slice(grp * 32, grp * 32 + 32)
        lens = jnp.zeros((32, 128), jnp.int32)
        for r in range(8):
            lens = jnp.where(row // NEW == r, len_ref[grp * 8 + r], lens)
        cos, sin = cos_sin((lens + row % NEW).astype(F32) * freq)
        sin = jnp.where(first, -sin, sin)
        tiles = [proj[rows, 128 * i : 128 * i + 128] for i in range(5)]
        turned = [t * cos + jnp.where(first, pltpu.roll(t, 96, 1), pltpu.roll(t, 32, 1)) * sin for t in tiles]
        query = []
        for g in range(2):
            for q in range(GROUP):
                at = g * 5 + q
                t = turned[at // 2]
                if at % 2 != g:
                    t = pltpu.roll(t, 64, 1)
                query.append(jnp.where(low if g == 0 else ~low, t * 0.125, 0.0).astype(BF16))
        qg = jnp.concatenate(query, axis=0)
        key_new = jnp.where(low, pltpu.roll(turned[1], 64, 1), pltpu.roll(turned[4], 64, 1)).astype(BF16)
        value_new = jnp.where(low, tiles[2], tiles[4]).astype(BF16)

        back = lens - 1 - slot
        safe = jnp.maximum(back, 0)
        age = safe - ((safe * 32833) >> 26) * WINDOW
        ok = (back >= 0) & ((slot < SINK) | (age <= WINDOW - 1 - row % NEW))
        ok = jnp.concatenate([ok & (row // NEW == lane // SLOTS + 4 * i) for i in range(2)], axis=1)
        s = dot_t(qg, k_ref[grp * 256 : grp * 256 + 256, :]).reshape(6, 32, 256)
        sn = dot_t(qg, key_new).reshape(6, 32, 32)
        s = jnp.where(ok[None], s, FLOOR_SCORE)
        sn = jnp.where(ok_new[None], sn, FLOOR_SCORE)
        m = jnp.maximum(jnp.max(s, axis=-1, keepdims=True), jnp.max(sn, axis=-1, keepdims=True))
        p = jnp.where(ok[None], jnp.exp(s - m), 0.0)
        pn = jnp.where(ok_new[None], jnp.exp(sn - m), 0.0)
        mass = jnp.sum(p, axis=-1, keepdims=True) + jnp.sum(pn, axis=-1, keepdims=True)
        acc = dot(p.reshape(192, 256).astype(BF16), v_ref[grp * 256 : grp * 256 + 256, :]) + dot(
            pn.reshape(192, 32).astype(BF16), value_new
        )
        some = mass > 0.0
        mass = jnp.where(some, mass, 1.0)
        acc = acc.reshape(6, 32, 128) / mass
        lse = jnp.where(some, m + jnp.log(mass), FLOOR_SCORE)
        for g in range(2):
            a = [acc[g * 3 + q] for q in range(3)]
            a = [b if q % 2 == g else pltpu.roll(b, 64, 1) for q, b in enumerate(a)]
            e = [lse[g * 3 + q] for q in range(3)]
            stats = jnp.where(lane == 64, e[0], jnp.where(lane == 65, e[1], jnp.where(lane == 66, e[2], 0.0)))
            lo, hi = encode(jnp.where(low, a[0], a[1]), a[2], stats)
            for c in range(2):
                out_ref[grp * 2 + c, :, 256 * g : 256 * g + 128] = lo[16 * c : 16 * c + 16]
                out_ref[grp * 2 + c, :, 256 * g + 128 : 256 * g + 256] = hi[16 * c : 16 * c + 16]


def merge(parts):
    top = functools.reduce(jnp.maximum, [e for _, _, e in parts])
    weights = [jnp.exp(e - top) for _, _, e in parts]
    total = sum(weights)
    lo = hi = 0.0
    glow = iota(total.shape, 1) < 64
    for w, (a, b, _) in zip(weights, parts):
        w = w / total
        lo = lo + a * jnp.where(glow, w[:, 64:65], w[:, 65:66])
        hi = hi + b * w[:, 66:67]
    return lo, hi, top + jnp.log(total)


def encode(lo, hi, lse):
    lane = iota(lse.shape, 1)
    a = lse.astype(BF16).astype(F32)
    b = (lse - a).astype(BF16).astype(F32)
    c = lse - a - b
    tail = jnp.where(lane < 67, a, jnp.where(lane < 70, pltpu.roll(b, 3, 1), pltpu.roll(c, 6, 1)))
    tail = jnp.where(lane < 73, tail, 0.0)
    return lo.astype(BF16), jnp.where(lane < 64, hi, tail).astype(BF16)


def decode(block):
    lo = block[:, :128].astype(F32)
    hi = block[:, 128:].astype(F32)
    lse = hi + pltpu.roll(hi, 125, 1) + pltpu.roll(hi, 122, 1)
    lane = iota(lse.shape, 1)
    return lo, hi, jnp.where((lane >= 64) & (lane < 67), lse, 0.0)


def merge_y_body(in_ref, out_ref):
    for g in range(2):
        at = slice(256 * g, 256 * g + 256)
        lo, hi = encode(*merge([decode(in_ref[i, :, at]) for i in range(8)]))
        for i in range(8):
            out_ref[i, :, 256 * g : 256 * g + 128] = lo
            out_ref[i, :, 256 * g + 128 : 256 * g + 256] = hi


def merge_z_body(in_ref, out_ref):
    heads = []
    for g in range(2):
        at = slice(256 * g, 256 * g + 256)
        heads.append(merge([decode(in_ref[i, :, at]) for i in range(8)]))
    low = iota((16, 128), 1) < 64
    last = jnp.where(low, heads[0][1], pltpu.roll(heads[1][1], 64, 1))
    for j, v in enumerate((heads[0][0], heads[1][0], last)):
        v = v.astype(BF16)
        for i in range(16):
            out_ref[i, :, 128 * j : 128 * j + 128] = v


def split3(v):
    a = v.astype(BF16)
    r = v - a.astype(F32)
    b = r.astype(BF16)
    return a, b, (r - b.astype(F32)).astype(BF16)


def own_rows(v, core):
    v = v.reshape(4, 32, v.shape[-1])
    return jnp.where(core == 0, v[:, :16], v[:, 16:]).reshape(HALF, v.shape[-1])


def project_body(
    mine_ref,
    w_ref,
    tok_ref,
    router_ref,
    routes_ref,
    gate1_ref,
    up1_ref,
    gain_hbm,
    gate0_hbm,
    up0_hbm,
    res_ref,
    out_ref,
    gate0_ref,
    up0_ref,
    gain_ref,
    sems,
):
    core = lax.axis_index("core")
    tp = lax.axis_index("tp")
    pairs = [(gate0_hbm, gate0_ref), (up0_hbm, up0_ref), (gain_hbm, gain_ref)]
    copies = started(pairs, sems)
    acc = jnp.zeros((HALF, FEAT), F32)
    for x in range(4):
        a = jnp.concatenate([mine_ref[y * 4 + x] for y in range(4)], axis=0)
        spans = [(0, 128), (192, 320), (128, 192), (320, 384)]
        w = jnp.concatenate([w_ref[384 * x + i : 384 * x + j, :] for i, j in spans], axis=0)
        acc = acc + dot(a, w)
    own = own_rows(tok_ref[:, pl.ds(pl.multiple_of(tp * FEAT, 128), FEAT)].astype(F32), core)
    acc = acc + own
    res_ref[...] = acc
    copies[2].wait()
    gained = acc * gain_ref[...].reshape(1, FEAT)
    squares = jnp.sum(acc * acc, axis=-1, keepdims=True)
    router = router_ref[...]
    g0, g1, g2 = split3(gained)
    logits = dot_t(g0, router) + dot_t(g1, router) + dot_t(g2, router)
    routes = own_rows(routes_ref[...].T, core)
    elane = iota((HALF, EXPERTS), 1)
    lane = iota((HALF, 128), 1)
    frow = iota((256, 128), 0)
    fcol = iota((256, 128), 1)
    fold = ((frow % FF == fcol % 64) & (frow // 128 == fcol // 64)).astype(BF16)
    stats = jnp.where(lane == TOP, squares, 0.0)
    for k in range(TOP):
        chosen = jnp.sum(jnp.where(elane == routes[:, k : k + 1], logits, 0.0), axis=-1, keepdims=True)
        stats = jnp.where(lane == k, chosen, stats)
    masks = [[lane // FF + 16 * i == routes[:, k : k + 1] for i in range(3)] for k in range(TOP)]
    blank = jnp.zeros((HALF, 64), F32)

    def picked(weight_ref):
        v = jnp.concatenate([dot_t(g0, weight_ref[...]), blank], axis=1)
        t = [v[:, 128 * i : 128 * i + 128] for i in range(3)]
        rows = [jnp.where(m[0], t[0], jnp.where(m[1], t[1], jnp.where(m[2], t[2], 0.0))) for m in masks]
        return jnp.concatenate([r.astype(BF16) for r in rows], axis=0)

    picks = []
    for gate_ref, up_ref in ((gate1_ref, up1_ref), (gate0_ref, up0_ref)):
        if gate_ref is gate0_ref:
            for c in copies[:2]:
                c.wait()
        v = jnp.concatenate([picked(gate_ref), picked(up_ref)], axis=1)
        v = dot(v, fold).reshape(TOP, HALF, 128)
        picks.insert(0, sum(v[k] if k == 0 else pltpu.roll(v[k], FF * k, 1) for k in range(TOP)))
    a, b, c = (v.astype(F32) for v in split3(stats))
    tail = (a + pltpu.roll(b, 16, 1) + pltpu.roll(c, 32, 1)).astype(BF16)
    for i in range(4):
        out_ref[i, :, :128] = picks[0].astype(BF16)
        out_ref[i, :, 128:256] = picks[1].astype(BF16)
        out_ref[i, :, 256:] = tail


def expert_body(in_ref, routes_ref, down1_ref, down0_hbm, out_ref, down0_ref, sems):
    core = lax.axis_index("core")
    copies = started([(down0_hbm, down0_ref)], sems)
    lane = iota((HALF, 128), 1)
    tail = sum(in_ref[i, :, 256:].astype(F32) for i in range(4))
    stats = tail + pltpu.roll(tail, 112, 1) + pltpu.roll(tail, 96, 1)
    scale = lax.rsqrt(stats[:, TOP : TOP + 1] / D + EPSILON)
    logits = jnp.where(lane < TOP, stats * scale, FLOOR_SCORE)
    weights = jnp.exp(logits - jnp.max(logits, axis=-1, keepdims=True))
    prob = weights / jnp.sum(weights, axis=-1, keepdims=True)
    wide = jnp.zeros((HALF, 128), F32)
    for k in range(TOP):
        wide = jnp.where(lane // FF == k, prob[:, k : k + 1], wide)
    erow = iota((128, 1024), 0)
    ecol = iota((128, 1024), 1)
    spread_to = ((erow % FF == ecol % FF) & (erow // FF == ecol // 128)).astype(BF16)
    tiled = []
    for j in range(2):
        gate = scale * sum(in_ref[i, :, 128 * j : 128 * j + 128].astype(F32) for i in range(4))
        up = pltpu.roll(gate, 64, 1)
        activated = (gate / (1.0 + jnp.exp(-gate)) * up).astype(BF16).astype(F32)
        tiled.append(dot(jnp.where(lane < 64, wide * activated, 0.0).astype(BF16), spread_to))
    routes = own_rows(routes_ref[...].T, core)
    part = jnp.zeros((HALF, FEAT), F32)
    for t, down_ref in zip(tiled[::-1], (down1_ref, down0_ref)):
        spread = []
        for i in range(3):
            s = jnp.zeros((HALF, 128), F32)
            for k in range(TOP):
                s = jnp.where(lane // FF + 16 * i == routes[:, k : k + 1], t[:, 128 * k : 128 * k + 128], s)
            spread.append(s)
        spread = jnp.concatenate(spread, axis=1)[:, :320].astype(BF16)
        if down_ref is down0_ref:
            copies[0].wait()
        part = part + dot(spread, down_ref[...])
    for i in range(8):
        out_ref[i] = part.astype(BF16)


def group_body(in_ref, out_ref):
    v = sum(in_ref[i].astype(F32) for i in range(8)).astype(BF16)
    for i in range(4):
        out_ref[i] = v


def finish_body(in_ref, res_ref, out_ref):
    out_ref[...] = (res_ref[...] + sum(in_ref[i].astype(F32) for i in range(4))).astype(BF16)


def assemble_body(own_ref, other_ref, out_ref):
    core = lax.axis_index("core")
    for y in range(4):
        rows = slice(16 * y, 16 * y + 16)
        out_ref[pl.ds(pl.multiple_of(y * 32 + core * 16, 16), 16), :] = own_ref[rows]
        out_ref[pl.ds(pl.multiple_of(y * 32 + (1 - core) * 16, 16), 16), :] = other_ref[rows]


def swap(v):
    return lax.ppermute(v, "core", [(0, 1), (1, 0)])


def exchange(v, axes):
    return lax.all_to_all(v, axes, 0, 0, tiled=True)


def on_device(
    tokens,
    attn_gain,
    qkv_weight,
    out_weight,
    moe_gain,
    router_weight,
    expert_gate,
    expert_up,
    expert_down,
    cache_keys,
    cache_values,
    lengths,
    routes,
):
    z = ("zh", "zl")
    units = EXPERTS * FF
    gate = expert_gate.transpose(0, 2, 1).reshape(units, FEAT)
    up = expert_up.transpose(0, 2, 1).reshape(units, FEAT)
    down = expert_down.reshape(units, FEAT)
    gate_there, up_there, down_there = swap(gate), swap(up), swap(down)
    (packed,) = call(
        attend_body,
        [((8, 16, 512), BF16)],
        (
            lengths,
            tokens,
            attn_gain,
            qkv_weight,
            cache_keys.reshape(REQS * SLOTS, 128),
            cache_values.reshape(REQS * SLOTS, 128),
        ),
        smem=(0,),
        raw=range(1, 6),
        scratch=[
            pltpu.VMEM((TOKENS, D), BF16),
            pltpu.VMEM((D,), F32),
            pltpu.VMEM((D, 640), BF16),
            pltpu.VMEM((REQS * SLOTS, 128), BF16),
            pltpu.VMEM((REQS * SLOTS, 128), BF16),
            pltpu.SemaphoreType.DMA((4 + CHUNKS,)),
        ],
    )
    packed, gate_there, up_there, down_there = lax.optimization_barrier((packed, gate_there, up_there, down_there))
    (packed,) = call(merge_y_body, [((8, 16, 512), BF16)], (exchange(packed, ("y", "core")),))
    (packed,) = call(merge_z_body, [((16, 16, 384), BF16)], (exchange(packed, z),))
    residual, picked = call(
        project_body,
        [((HALF, FEAT), F32), ((4, HALF, 384), BF16)],
        (
            exchange(packed, ("y", "tp")),
            out_weight,
            tokens,
            router_weight.T,
            routes.T,
            gate_there,
            up_there,
            moe_gain,
            gate,
            up,
        ),
        raw=(7, 8, 9),
        scratch=[pltpu.VMEM((units, FEAT), BF16)] * 2 + [pltpu.VMEM((FEAT,), F32), pltpu.SemaphoreType.DMA((3,))],
    )
    (part,) = call(
        expert_body,
        [((8, HALF, FEAT), BF16)],
        (exchange(picked, "tp"), routes.T, down_there, down),
        raw=(3,),
        scratch=[pltpu.VMEM((units, FEAT), BF16), pltpu.SemaphoreType.DMA((1,))],
    )
    (part,) = call(group_body, [((4, HALF, FEAT), BF16)], (exchange(part, ("zl", "y")),))
    (own,) = call(finish_body, [((HALF, FEAT), BF16)], (exchange(part, "zh"), residual))
    (out,) = call(assemble_body, [((TOKENS, FEAT), BF16)], (own, swap(own)), pinned=False)
    return out


def solution(mesh):
    seq = ("zh", "zl", "y", "core")
    grid = Mesh(mesh.devices.reshape(4, 2, 4, 2, 4), seq + ("tp",))
    in_specs = (
        P(),
        P(),
        P(None, "tp"),
        P(None, "tp"),
        P("tp"),
        P("tp", None),
        P(None, "tp", seq),
        P(None, "tp", seq),
        P(None, seq, "tp"),
        P(None, seq, "tp"),
        P(None, seq, "tp"),
        P(),
        P(),
    )
    out_specs = P(None, "tp")
    return jax.shard_map(on_device, mesh=grid, in_specs=in_specs, out_specs=out_specs, check_vma=False)
```

```python
import functools

import jax
import jax.numpy as jnp
import numpy as np
from jax import lax
from jax.experimental import pallas as pl
from jax.experimental.pallas import tpu as pltpu
from jax.sharding import Mesh, PartitionSpec as P

D = 1536
HEAD = 64
EXPERTS = 40
TOP = 8
SINK = 4
NEW = 4
GROUP = 3
REQS = 32
TOKENS = 128
WINDOW = 2044
SLOTS = 32
FEAT = 384
FF = 8
CHUNKS = 4
HALF = TOKENS // 2

EPSILON = 1e-06
ROPE_BASE = 10000.0
FLOOR_SCORE = -1e30

F32 = jnp.float32
BF16 = jnp.bfloat16
VMEM = pl.BlockSpec(memory_space=pltpu.VMEM)
SMEM = pl.BlockSpec(memory_space=pltpu.SMEM)


def iota(shape, dim):
    return lax.broadcasted_iota(jnp.int32, shape, dim)


def dot(a, b):
    return jnp.dot(a, b, preferred_element_type=F32)


def dot_t(a, b):
    return lax.dot_general(a, b, (((1,), (1,)), ((), ())), preferred_element_type=F32)


def call(body, outs, args, smem=(), raw=(), scratch=(), pinned=True):
    kinds = ["s" if i in smem else "r" if i in raw else "v" for i in range(len(args))]
    run = pl.pallas_call(
        body,
        out_shape=[(pltpu.VMEM if pinned else jax.ShapeDtypeStruct)(shape, dtype) for shape, dtype in outs],
        in_specs=[{"s": SMEM, "r": pl.BlockSpec(memory_space=pl.ANY), "v": VMEM}[k] for k in kinds],
        out_specs=[VMEM for _ in outs],
        scratch_shapes=list(scratch),
        cost_estimate=pl.CostEstimate(flops=10**7, bytes_accessed=10**6, transcendentals=0),
    )
    space = {"s": pltpu.MemorySpace.SMEM, "r": pl.ANY, "v": pltpu.MemorySpace.VMEM}
    return run(*[pltpu.with_memory_space_constraint(a, space[k]) for a, k in zip(args, kinds)])


def started(pairs, sems):
    copies = [pltpu.make_async_copy(src, dst, sems.at[i]) for i, (src, dst) in enumerate(pairs)]
    for c in copies:
        c.start()
    return copies


def cos_sin(angle):
    turns = jnp.floor(angle * (2.0 / np.pi) + 0.5)
    r = angle - turns * QUARTER[0]
    r = r - turns * QUARTER[1]
    r = r - turns * QUARTER[2]
    r = r - turns * QUARTER[3]
    r2 = r * r
    sin = r + r * r2 * (-1.0 / 6 + r2 * (1.0 / 120 + r2 * (-1.0 / 5040 + r2 * (1.0 / 362880))))
    cos = 1.0 - 0.5 * r2 + r2 * r2 * (1.0 / 24 + r2 * (-1.0 / 720 + r2 * (1.0 / 40320 - r2 * (1.0 / 3628800))))
    which = turns.astype(jnp.int32) & 3
    odd = (which & 1) == 1
    c = jnp.where(odd, sin, cos)
    s = jnp.where(odd, cos, sin)
    return jnp.where((which == 1) | (which == 2), -c, c), jnp.where(which >= 2, -s, s)


def quarter_pieces():
    pieces = []
    rest = np.pi / 2
    for _ in range(3):
        top = np.floor(rest * 2.0 ** (7 - np.floor(np.log2(rest)))) / 2.0 ** (7 - np.floor(np.log2(rest)))
        pieces.append(float(top))
        rest = rest - top
    return pieces + [float(np.float32(rest))]


QUARTER = quarter_pieces()


def attend_body(
    len_ref,
    tok_hbm,
    gain_hbm,
    w_hbm,
    k_hbm,
    v_hbm,
    out_ref,
    tok_ref,
    gain_ref,
    w_ref,
    k_ref,
    v_ref,
    sems,
):
    part = D // CHUNKS
    pairs = [(tok_hbm, tok_ref), (gain_hbm, gain_ref)]
    pairs += [(w_hbm.at[pl.ds(i * part, part)], w_ref.at[pl.ds(i * part, part)]) for i in range(CHUNKS)]
    pairs += [(k_hbm, k_ref), (v_hbm, v_ref)]
    copies = started(pairs, sems)
    seq = ((lax.axis_index("zh") * 2 + lax.axis_index("zl")) * 4 + lax.axis_index("y")) * 2 + lax.axis_index("core")
    half = HEAD // 2
    spot = iota((8, 128), 1) % half
    freq = jnp.zeros((8, 128), F32)
    for i in range(half):
        freq = jnp.where(spot == i, float(np.float32(ROPE_BASE ** (-i / half))), freq)
    freq = freq[:1]
    copies[0].wait()
    copies[1].wait()
    x = tok_ref[...].astype(F32)
    normed = x * lax.rsqrt(jnp.mean(x * x, axis=-1, keepdims=True) + EPSILON) * gain_ref[...].reshape(1, D)
    normed = normed.astype(BF16)
    proj = jnp.zeros((TOKENS, 640), F32)
    for i in range(CHUNKS):
        copies[2 + i].wait()
        proj = proj + dot(normed[:, i * part : (i + 1) * part], w_ref[i * part : (i + 1) * part, :])
    copies[2 + CHUNKS].wait()
    copies[3 + CHUNKS].wait()
    lane = iota((32, 128), 1)
    row = iota((32, 128), 0)
    low = lane < 64
    first = (lane % 64) < 32
    slot = seq * SLOTS + lane % SLOTS
    nrow = iota((32, 32), 0)
    ncol = iota((32, 32), 1)
    ok_new = (nrow // NEW == ncol // NEW) & (ncol <= nrow) & (seq == 0)
    for grp in range(4):
        rows = slice(grp * 32, grp * 32 + 32)
        lens = jnp.zeros((32, 128), jnp.int32)
        for r in range(8):
            lens = jnp.where(row // NEW == r, len_ref[grp * 8 + r], lens)
        cos, sin = cos_sin((lens + row % NEW).astype(F32) * freq)
        sin = jnp.where(first, -sin, sin)
        tiles = [proj[rows, 128 * i : 128 * i + 128] for i in range(5)]
        turned = [t * cos + jnp.where(first, pltpu.roll(t, 96, 1), pltpu.roll(t, 32, 1)) * sin for t in tiles]
        query = []
        for g in range(2):
            for q in range(GROUP):
                at = g * 5 + q
                t = turned[at // 2]
                if at % 2 != g:
                    t = pltpu.roll(t, 64, 1)
                query.append(jnp.where(low if g == 0 else ~low, t * 0.125, 0.0).astype(BF16))
        qg = jnp.concatenate(query, axis=0)
        key_new = jnp.where(low, pltpu.roll(turned[1], 64, 1), pltpu.roll(turned[4], 64, 1)).astype(BF16)
        value_new = jnp.where(low, tiles[2], tiles[4]).astype(BF16)

        back = lens - 1 - slot
        safe = jnp.maximum(back, 0)
        age = safe - ((safe * 32833) >> 26) * WINDOW
        ok = (back >= 0) & ((slot < SINK) | (age <= WINDOW - 1 - row % NEW))
        ok = jnp.concatenate([ok & (row // NEW == lane // SLOTS + 4 * i) for i in range(2)], axis=1)
        s = dot_t(qg, k_ref[grp * 256 : grp * 256 + 256, :]).reshape(6, 32, 256)
        sn = dot_t(qg, key_new).reshape(6, 32, 32)
        s = jnp.where(ok[None], s, FLOOR_SCORE)
        sn = jnp.where(ok_new[None], sn, FLOOR_SCORE)
        m = jnp.maximum(jnp.max(s, axis=-1, keepdims=True), jnp.max(sn, axis=-1, keepdims=True))
        m = jnp.maximum(m, 0.1 * FLOOR_SCORE)
        p = jnp.exp(s - m)
        pn = jnp.exp(sn - m)
        mass = jnp.sum(p, axis=-1, keepdims=True) + jnp.sum(pn, axis=-1, keepdims=True)
        acc = dot(p.reshape(192, 256).astype(BF16), v_ref[grp * 256 : grp * 256 + 256, :]) + dot(
            pn.reshape(192, 32).astype(BF16), value_new
        )
        some = mass > 0.0
        mass = jnp.where(some, mass, 1.0)
        acc = acc.reshape(6, 32, 128) / mass
        lse = jnp.where(some, m + jnp.log(mass), FLOOR_SCORE)
        for g in range(2):
            a = [acc[g * 3 + q] for q in range(3)]
            a = [b if q % 2 == g else pltpu.roll(b, 64, 1) for q, b in enumerate(a)]
            e = [lse[g * 3 + q] for q in range(3)]
            stats = jnp.where(lane == 64, e[0], jnp.where(lane == 65, e[1], jnp.where(lane == 66, e[2], 0.0)))
            lo, hi = encode(jnp.where(low, a[0], a[1]), a[2], stats)
            for c in range(2):
                out_ref[grp * 2 + c, :, 256 * g : 256 * g + 128] = lo[16 * c : 16 * c + 16]
                out_ref[grp * 2 + c, :, 256 * g + 128 : 256 * g + 256] = hi[16 * c : 16 * c + 16]


def merge(parts):
    top = functools.reduce(jnp.maximum, [e for _, _, e in parts])
    weights = [jnp.exp(e - top) for _, _, e in parts]
    total = sum(weights)
    lo = hi = 0.0
    glow = iota(total.shape, 1) < 64
    for w, (a, b, _) in zip(weights, parts):
        w = w / total
        lo = lo + a * jnp.where(glow, w[:, 64:65], w[:, 65:66])
        hi = hi + b * w[:, 66:67]
    return lo, hi, top + jnp.log(total)


def encode(lo, hi, lse):
    lane = iota(lse.shape, 1)
    a = lse.astype(BF16).astype(F32)
    b = (lse - a).astype(BF16).astype(F32)
    c = lse - a - b
    tail = jnp.where(lane < 67, a, jnp.where(lane < 70, pltpu.roll(b, 3, 1), pltpu.roll(c, 6, 1)))
    tail = jnp.where(lane < 73, tail, 0.0)
    return lo.astype(BF16), jnp.where(lane < 64, hi, tail).astype(BF16)


def decode(block):
    lo = block[:, :128].astype(F32)
    hi = block[:, 128:].astype(F32)
    lse = hi + pltpu.roll(hi, 125, 1) + pltpu.roll(hi, 122, 1)
    lane = iota(lse.shape, 1)
    return lo, hi, jnp.where((lane >= 64) & (lane < 67), lse, 0.0)


def merge_y_body(in_ref, out_ref):
    for g in range(2):
        at = slice(256 * g, 256 * g + 256)
        lo, hi = encode(*merge([decode(in_ref[i, :, at]) for i in range(8)]))
        for i in range(8):
            out_ref[i, :, 256 * g : 256 * g + 128] = lo
            out_ref[i, :, 256 * g + 128 : 256 * g + 256] = hi


def merge_z_body(in_ref, out_ref):
    heads = []
    for g in range(2):
        at = slice(256 * g, 256 * g + 256)
        heads.append(merge([decode(in_ref[i, :, at]) for i in range(8)]))
    low = iota((16, 128), 1) < 64
    last = jnp.where(low, heads[0][1], pltpu.roll(heads[1][1], 64, 1))
    for j, v in enumerate((heads[0][0], heads[1][0], last)):
        v = v.astype(BF16)
        for i in range(16):
            out_ref[i, :, 128 * j : 128 * j + 128] = v


def split3(v):
    a = v.astype(BF16)
    r = v - a.astype(F32)
    b = r.astype(BF16)
    return a, b, (r - b.astype(F32)).astype(BF16)


def own_rows(v, core):
    v = v.reshape(4, 32, v.shape[-1])
    return jnp.where(core == 0, v[:, :16], v[:, 16:]).reshape(HALF, v.shape[-1])


def project_body(
    mine_ref,
    w_ref,
    tok_ref,
    router_ref,
    routes_ref,
    gate1_ref,
    up1_ref,
    gain_hbm,
    gate0_hbm,
    up0_hbm,
    res_ref,
    out_ref,
    gate0_ref,
    up0_ref,
    gain_ref,
    sems,
):
    core = lax.axis_index("core")
    tp = lax.axis_index("tp")
    pairs = [(gate0_hbm, gate0_ref), (up0_hbm, up0_ref), (gain_hbm, gain_ref)]
    copies = started(pairs, sems)
    acc = jnp.zeros((HALF, FEAT), F32)
    for x in range(4):
        a = jnp.concatenate([mine_ref[y * 4 + x] for y in range(4)], axis=0)
        spans = [(0, 128), (192, 320), (128, 192), (320, 384)]
        w = jnp.concatenate([w_ref[384 * x + i : 384 * x + j, :] for i, j in spans], axis=0)
        acc = acc + dot(a, w)
    own = own_rows(tok_ref[:, pl.ds(pl.multiple_of(tp * FEAT, 128), FEAT)].astype(F32), core)
    acc = acc + own
    res_ref[...] = acc
    copies[2].wait()
    gained = acc * gain_ref[...].reshape(1, FEAT)
    squares = jnp.sum(acc * acc, axis=-1, keepdims=True)
    router = router_ref[...]
    g0, g1, g2 = split3(gained)
    logits = dot_t(g0, router) + dot_t(g1, router) + dot_t(g2, router)
    routes = own_rows(routes_ref[...].T, core)
    elane = iota((HALF, EXPERTS), 1)
    lane = iota((HALF, 128), 1)
    frow = iota((256, 128), 0)
    fcol = iota((256, 128), 1)
    fold = ((frow % FF == fcol % 64) & (frow // 128 == fcol // 64)).astype(BF16)
    stats = jnp.where(lane == TOP, squares, 0.0)
    for k in range(TOP):
        chosen = jnp.sum(jnp.where(elane == routes[:, k : k + 1], logits, 0.0), axis=-1, keepdims=True)
        stats = jnp.where(lane == k, chosen, stats)
    masks = [[lane // FF + 16 * i == routes[:, k : k + 1] for i in range(3)] for k in range(TOP)]
    blank = jnp.zeros((HALF, 64), F32)

    def picked(weight_ref):
        v = jnp.concatenate([dot_t(g0, weight_ref[...]), blank], axis=1)
        t = [v[:, 128 * i : 128 * i + 128] for i in range(3)]
        rows = [jnp.where(m[0], t[0], jnp.where(m[1], t[1], jnp.where(m[2], t[2], 0.0))) for m in masks]
        return jnp.concatenate([r.astype(BF16) for r in rows], axis=0)

    picks = []
    for gate_ref, up_ref in ((gate1_ref, up1_ref), (gate0_ref, up0_ref)):
        if gate_ref is gate0_ref:
            for c in copies[:2]:
                c.wait()
        v = jnp.concatenate([picked(gate_ref), picked(up_ref)], axis=1)
        v = dot(v, fold).reshape(TOP, HALF, 128)
        picks.insert(0, sum(v[k] if k == 0 else pltpu.roll(v[k], FF * k, 1) for k in range(TOP)))
    a, b, c = (v.astype(F32) for v in split3(stats))
    tail = (a + pltpu.roll(b, 16, 1) + pltpu.roll(c, 32, 1)).astype(BF16)
    for i in range(4):
        out_ref[i, :, :128] = picks[0].astype(BF16)
        out_ref[i, :, 128:256] = picks[1].astype(BF16)
        out_ref[i, :, 256:] = tail


def expert_body(in_ref, routes_ref, down1_ref, down0_hbm, out_ref, down0_ref, sems):
    core = lax.axis_index("core")
    copies = started([(down0_hbm, down0_ref)], sems)
    lane = iota((HALF, 128), 1)
    tail = sum(in_ref[i, :, 256:].astype(F32) for i in range(4))
    stats = tail + pltpu.roll(tail, 112, 1) + pltpu.roll(tail, 96, 1)
    scale = lax.rsqrt(stats[:, TOP : TOP + 1] / D + EPSILON)
    logits = jnp.where(lane < TOP, stats * scale, FLOOR_SCORE)
    weights = jnp.exp(logits - jnp.max(logits, axis=-1, keepdims=True))
    prob = weights / jnp.sum(weights, axis=-1, keepdims=True)
    wide = jnp.zeros((HALF, 128), F32)
    for k in range(TOP):
        wide = jnp.where(lane // FF == k, prob[:, k : k + 1], wide)
    erow = iota((128, 1024), 0)
    ecol = iota((128, 1024), 1)
    spread_to = ((erow % FF == ecol % FF) & (erow // FF == ecol // 128)).astype(BF16)
    tiled = []
    for j in range(2):
        gate = scale * sum(in_ref[i, :, 128 * j : 128 * j + 128].astype(F32) for i in range(4))
        up = pltpu.roll(gate, 64, 1)
        activated = (gate / (1.0 + jnp.exp(-gate)) * up).astype(BF16).astype(F32)
        tiled.append(dot(jnp.where(lane < 64, wide * activated, 0.0).astype(BF16), spread_to))
    routes = own_rows(routes_ref[...].T, core)
    part = jnp.zeros((HALF, FEAT), F32)
    for t, down_ref in zip(tiled[::-1], (down1_ref, down0_ref)):
        spread = []
        for i in range(3):
            s = jnp.zeros((HALF, 128), F32)
            for k in range(TOP):
                s = jnp.where(lane // FF + 16 * i == routes[:, k : k + 1], t[:, 128 * k : 128 * k + 128], s)
            spread.append(s)
        spread = jnp.concatenate(spread, axis=1)[:, :320].astype(BF16)
        if down_ref is down0_ref:
            copies[0].wait()
        part = part + dot(spread, down_ref[...])
    for i in range(4):
        out_ref[i] = part.astype(BF16)


def group_body(in_ref, out_ref):
    v = sum(in_ref[i].astype(F32) for i in range(4)).astype(BF16)
    for i in range(8):
        out_ref[i] = v


def finish_body(in_ref, res_ref, out_ref):
    out_ref[...] = (res_ref[...] + sum(in_ref[i].astype(F32) for i in range(8))).astype(BF16)


def assemble_body(own_ref, other_ref, out_ref):
    core = lax.axis_index("core")
    for y in range(4):
        rows = slice(16 * y, 16 * y + 16)
        out_ref[pl.ds(pl.multiple_of(y * 32 + core * 16, 16), 16), :] = own_ref[rows]
        out_ref[pl.ds(pl.multiple_of(y * 32 + (1 - core) * 16, 16), 16), :] = other_ref[rows]


def swap(v):
    return lax.ppermute(v, "core", [(0, 1), (1, 0)])


def exchange(v, axes):
    return lax.all_to_all(v, axes, 0, 0, tiled=True)


def on_device(
    tokens,
    attn_gain,
    qkv_weight,
    out_weight,
    moe_gain,
    router_weight,
    expert_gate,
    expert_up,
    expert_down,
    cache_keys,
    cache_values,
    lengths,
    routes,
):
    z = ("zh", "zl")
    units = EXPERTS * FF
    gate = expert_gate.transpose(0, 2, 1).reshape(units, FEAT)
    up = expert_up.transpose(0, 2, 1).reshape(units, FEAT)
    down = expert_down.reshape(units, FEAT)
    gate_there, up_there, down_there = swap(gate), swap(up), swap(down)
    (packed,) = call(
        attend_body,
        [((8, 16, 512), BF16)],
        (
            lengths,
            tokens,
            attn_gain,
            qkv_weight,
            cache_keys.reshape(REQS * SLOTS, 128),
            cache_values.reshape(REQS * SLOTS, 128),
        ),
        smem=(0,),
        raw=range(1, 6),
        scratch=[
            pltpu.VMEM((TOKENS, D), BF16),
            pltpu.VMEM((D,), F32),
            pltpu.VMEM((D, 640), BF16),
            pltpu.VMEM((REQS * SLOTS, 128), BF16),
            pltpu.VMEM((REQS * SLOTS, 128), BF16),
            pltpu.SemaphoreType.DMA((4 + CHUNKS,)),
        ],
    )
    packed, gate_there, up_there, down_there = lax.optimization_barrier((packed, gate_there, up_there, down_there))
    (packed,) = call(merge_y_body, [((8, 16, 512), BF16)], (exchange(packed, ("y", "core")),))
    (packed,) = call(merge_z_body, [((16, 16, 384), BF16)], (exchange(packed, z),))
    residual, picked = call(
        project_body,
        [((HALF, FEAT), F32), ((4, HALF, 384), BF16)],
        (
            exchange(packed, ("y", "tp")),
            out_weight,
            tokens,
            router_weight.T,
            routes.T,
            gate_there,
            up_there,
            moe_gain,
            gate,
            up,
        ),
        raw=(7, 8, 9),
        scratch=[pltpu.VMEM((units, FEAT), BF16)] * 2 + [pltpu.VMEM((FEAT,), F32), pltpu.SemaphoreType.DMA((3,))],
    )
    (part,) = call(
        expert_body,
        [((4, HALF, FEAT), BF16)] ,
        (exchange(picked, "tp"), routes.T, down_there, down),
        raw=(3,),
        scratch=[pltpu.VMEM((units, FEAT), BF16), pltpu.SemaphoreType.DMA((1,))],
    )
    (part,) = call(group_body, [((8, HALF, FEAT), BF16)], (exchange(part, "zh"),))
    (own,) = call(finish_body, [((HALF, FEAT), BF16)], (exchange(part, ("zl", "y")), residual))
    (out,) = call(assemble_body, [((TOKENS, FEAT), BF16)], (own, swap(own)), pinned=False)
    return out


def solution(mesh):
    seq = ("zh", "zl", "y", "core")
    grid = Mesh(mesh.devices.reshape(4, 2, 4, 2, 4), seq + ("tp",))
    in_specs = (
        P(),
        P(),
        P(None, "tp"),
        P(None, "tp"),
        P("tp"),
        P("tp", None),
        P(None, "tp", seq),
        P(None, "tp", seq),
        P(None, seq, "tp"),
        P(None, seq, "tp"),
        P(None, seq, "tp"),
        P(),
        P(),
    )
    out_specs = P(None, "tp")
    return jax.shard_map(on_device, mesh=grid, in_specs=in_specs, out_specs=out_specs, check_vma=False)
```
